256 devices in a mesh: ctx: 16 (over y, x), tp: 16 (over z, core).
Axes of the slice: x: 4, y: 4, z: 8, core: 2. Of those that a mesh axis runs over, the one named last changes fastest.
Arguments:
- queries: bfloat16 [3584, 8192], P('ctx', 'tp'), may hold values from -8 to 8
- keys: bfloat16 [3584, 1024], P('ctx'), may hold values from -8 to 8
- values: bfloat16 [3584, 1024], P('ctx'), may hold values from -32 to 32
- out_weight: bfloat16 [8192, 8192], P('tp'), may hold values from -0.09375 to 0.09375
- signs: int32 [8192], replicated, may hold values from 0 to 1
Outputs:
- rotated_payload: bfloat16 [3584, 8192], P('ctx')
- block_scales: float32 [3584, 64], P('ctx')
The draws below stay inside these ranges and needn't reach their ends.
All inputs are finite; a program needn't handle non-finite values. Where the reference program divides by a largest or mean magnitude, that divisor is 1e-20 or more.
Results may differ from the reference program's by a relative error of at most 0.0095.
Values may be sent and summed in bfloat16 or wider, within the bound.
No kernel may reach another device: no remote copies, remote signals or barrier semaphores. Data moves between devices by JAX's collectives and lax.ppermute only.
A program may use at most 128 MiB of HBM per device.

```python
import math
import jax
import jax.numpy as jnp
from jax import lax

D = 8192
QUERY_HEADS = 64
KEY_VALUE_HEADS = 8
HEAD_SIZE = 128
BLOCK = 128
SEQUENCE_TOKENS = 3584
N_TP = 16


def draw_queries(key, part):
    sampled_values = jnp.clip(jax.random.normal(jax.random.fold_in(key, 1), (SEQUENCE_TOKENS, QUERY_HEADS * HEAD_SIZE), jnp.float32), -6.0, 6.0)
    return sampled_values.astype(jnp.bfloat16)


def draw_keys(key, part):
    sampled_values = jnp.clip(jax.random.normal(jax.random.fold_in(key, 2), (SEQUENCE_TOKENS, KEY_VALUE_HEADS * HEAD_SIZE), jnp.float32), -6.0, 6.0)
    return sampled_values.astype(jnp.bfloat16)


def draw_values(key, part):
    sampled_values = jnp.clip(jax.random.normal(jax.random.fold_in(key, 3), (SEQUENCE_TOKENS, KEY_VALUE_HEADS * HEAD_SIZE), jnp.float32), -4.0, 4.0)
    return sampled_values.astype(jnp.bfloat16)


def plant(entries, key, least, largest):
    shape = entries.shape
    index_at = [jax.random.randint(jax.random.fold_in(key, axis), (), 0, shape[axis]) for axis in range(len(shape))]
    entries = entries.at[tuple(index_at)].set(least)
    longest = shape.index(max(shape))
    index_at[longest] = (index_at[longest] + 1) % shape[longest]
    return entries.at[tuple(index_at)].set(largest)


def spiked(values, own_key, source, target, shards_of, factor):
    owner, partner = [(jnp.arange(values.shape[position]) // (values.shape[position] // shards_of)).reshape([-1 if axis == position else 1 for axis in range(values.ndim)]) for position in (source, target)]
    chosen = jax.random.permutation(own_key, shards_of)[partner]
    strong = (owner == chosen) | (owner == (partner + shards_of // 2) % shards_of)
    return jnp.where(strong, factor * values, values)


def steps_of(stream_key, extent, split, low, largest):
    level, own = 1.0, jax.random.fold_in(stream_key, 6)
    for dim, shards_of in split:
        draws = jnp.exp(jax.random.uniform(jax.random.fold_in(own, dim), (shards_of,), jnp.float32, low / len(split), largest / len(split)))
        level = level * jnp.repeat(draws, extent[dim] // shards_of).reshape([-1 if axis == dim else 1 for axis in range(len(extent))])
    return level


def noise_with(key, shape, deviation, reach, cuts, heavy, kind=jnp.bfloat16):
    result = deviation * jax.random.normal(key, shape, jnp.float32)
    if cuts:
        result = result * steps_of(key, shape, cuts, -0.22, 0.18)
    return jnp.clip(spiked(result, jax.random.fold_in(key, 3), *heavy), -reach, reach).astype(kind)


def setup_inputs(seed: int = 0) -> dict:
    key_list = jax.random.split(jax.random.key(seed), 6)
    queries = draw_queries(jax.random.fold_in(key_list[5], 71), 0)
    keys = draw_keys(jax.random.fold_in(key_list[5], 71), 0)
    values = draw_values(jax.random.fold_in(key_list[5], 71), 0)
    out_weight = noise_with(key_list[3], (QUERY_HEADS * HEAD_SIZE, D), (QUERY_HEADS * HEAD_SIZE) ** -0.5, 0.09375, ((0, 16),), (0, 1, 16, 2.0))
    signs = plant(jax.random.randint(key_list[4], (D,), 0, 2), jax.random.fold_in(key_list[4], 1), 0, 1).astype(jnp.int32)
    return dict(queries=queries, keys=keys, values=values, out_weight=out_weight, signs=signs)


clip_ratio = 2.0

def hadamard():
    indices = jnp.arange(BLOCK, dtype=jnp.int32)
    common = jnp.bitwise_and(indices[:, None], indices[None, :])
    parity = jnp.zeros((BLOCK, BLOCK), jnp.int32)
    for bit_index in range(BLOCK.bit_length() - 1):
        parity = parity + jnp.bitwise_and(jnp.right_shift(common, bit_index), 1)
    signed = (1 - 2 * (parity % 2)).astype(jnp.float32)
    return signed * jnp.float32(1.0 / math.sqrt(BLOCK))

def rotate(partial_value, sign_row):
    row_count = partial_value.shape[0]
    flat = (partial_value * sign_row[None, :]).reshape(-1, BLOCK)
    turned = jnp.dot(flat, hadamard(), precision=lax.Precision.HIGHEST)
    return turned.reshape(row_count, D)

def clip_quantize(rotated):
    row_count = rotated.shape[0]
    blocked = rotated.reshape(row_count, -1, BLOCK)
    scales = clip_ratio * jnp.sqrt(lax.optimization_barrier(jnp.mean(blocked * blocked, axis=-1)) + 1e-06)
    payload = jnp.clip(blocked / scales[..., None], -1.0, 1.0).astype(jnp.bfloat16).reshape(row_count, -1)
    return (payload, scales)

def quantize(rotated):
    row_count = rotated.shape[0]
    blocked = rotated.reshape(row_count, -1, BLOCK)
    scales = lax.optimization_barrier(jnp.max(jnp.abs(blocked), axis=-1)) + 1e-06
    payload = (blocked / scales[..., None]).astype(jnp.bfloat16).reshape(row_count, -1)
    return (payload, scales)

def reference(queries, keys, values, out_weight, signs):
    score_scale = 1.0 / math.sqrt(HEAD_SIZE)
    group_width = QUERY_HEADS // KEY_VALUE_HEADS
    positions = jnp.arange(SEQUENCE_TOKENS, dtype=jnp.int32)
    allowed = positions[None, :] <= positions[:, None]
    query_heads = queries.reshape(SEQUENCE_TOKENS, QUERY_HEADS, HEAD_SIZE)
    key_head_count = keys.reshape(SEQUENCE_TOKENS, KEY_VALUE_HEADS, HEAD_SIZE)
    value_head_count = values.reshape(SEQUENCE_TOKENS, KEY_VALUE_HEADS, HEAD_SIZE)

    def one_head(head_index):
        kv_index = head_index // group_width
        query_one = lax.dynamic_index_in_dim(query_heads, head_index, 1, keepdims=False)
        key_one = lax.dynamic_index_in_dim(key_head_count, kv_index, 1, keepdims=False)
        value_one = lax.dynamic_index_in_dim(value_head_count, kv_index, 1, keepdims=False)
        scores = jnp.dot(query_one, key_one.T, preferred_element_type=jnp.float32) * score_scale
        scores = jnp.where(allowed, scores, -1e+30)
        row_max = lax.optimization_barrier(jnp.max(scores, axis=-1, keepdims=True))
        weights = jnp.where(allowed, jnp.exp(scores - row_max), 0.0)
        row_sum = lax.optimization_barrier(jnp.sum(weights, axis=-1, keepdims=True))
        mixed = jnp.dot(weights, value_one.astype(jnp.float32), precision=lax.Precision.HIGHEST)
        return (mixed / row_sum).astype(jnp.bfloat16)
    stacked = lax.map(one_head, jnp.arange(QUERY_HEADS, dtype=jnp.int32))
    attended = jnp.transpose(stacked, (1, 0, 2)).reshape(SEQUENCE_TOKENS, QUERY_HEADS * HEAD_SIZE)
    sign_row = (2 * signs - 1).astype(jnp.float32)
    group_cols = QUERY_HEADS * HEAD_SIZE // N_TP

    def add_group(tp_index, summed):
        start_col = (tp_index * group_cols).astype(jnp.int32)
        attended_part = lax.dynamic_slice_in_dim(attended, start_col, group_cols, 1)
        weight_part = lax.dynamic_slice_in_dim(out_weight, start_col, group_cols, 0)
        partial_value = jnp.dot(attended_part, weight_part, preferred_element_type=jnp.float32)
        payload, scales = clip_quantize(rotate(partial_value, sign_row))
        restored = payload.astype(jnp.float32).reshape(SEQUENCE_TOKENS, -1, BLOCK) * scales[..., None]
        return summed + restored.reshape(SEQUENCE_TOKENS, D)
    summed = lax.fori_loop(0, N_TP, add_group, jnp.zeros((SEQUENCE_TOKENS, D), jnp.float32))
    rotated_payload, block_scales = quantize(summed)
    return (rotated_payload, block_scales)
```

```python
import math

import jax
import jax.numpy as jnp
from jax import lax
from jax.experimental import pallas as pl
from jax.experimental.pallas import tpu as pltpu
from jax.sharding import PartitionSpec as P

D = 8192
HEAD = 128
BLOCK = 128
CHIPS = 8
TOKENS = 224
HALF = TOKENS // 2
HEADS = 4
KEYS = 3584
KEY_BLOCK = 512
CHUNK = D // CHIPS
COLS = 512
SUB = COLS // BLOCK
ROWS = SUB * HALF
MSG = ROWS + 16

UP = [(t, (t + 2) % 16) for t in range(16)]
DOWN = [(t, (t - 2) % 16) for t in range(16)]
PAIR = [(t, t ^ 1) for t in range(16)]


def plus_minus():
    indices = jnp.arange(BLOCK, dtype=jnp.int32)
    common = jnp.bitwise_and(indices[:, None], indices[None, :])
    parity = jnp.zeros((BLOCK, BLOCK), jnp.int32)
    for bit_index in range(BLOCK.bit_length() - 1):
        parity = parity + jnp.bitwise_and(jnp.right_shift(common, bit_index), 1)
    return (1 - 2 * (parity % 2)).astype(jnp.bfloat16)


def twice(matrix):
    zero = jnp.zeros_like(matrix)
    return jnp.concatenate(
        [jnp.concatenate([matrix, zero], 1), jnp.concatenate([zero, matrix], 1)], 0
    )


GROUP = HEADS * HALF


def attention_kernel(first_ref, q_ref, k_ref, v_ref, o_ref, wide, scores):
    first = first_ref[0]
    whole = first // KEY_BLOCK
    blocks = (first + HALF - 1) // KEY_BLOCK + 1
    gain = math.log2(math.e) / math.sqrt(HEAD)
    wide[:, :HEAD] = v_ref[...]
    wide[:, HEAD:] = jnp.ones((KEYS, HEAD), jnp.bfloat16)
    query_pos = first + lax.rem(
        lax.broadcasted_iota(jnp.int32, (GROUP, KEY_BLOCK), 0), HALF
    )
    key_pos = lax.broadcasted_iota(jnp.int32, (GROUP, KEY_BLOCK), 1)
    for group in range(2):
        rows = jnp.concatenate(
            [q_ref[group, :, h * HEAD : (h + 1) * HEAD] for h in range(HEADS)], 0
        )

        def fold(best, part):
            for t in range(KEY_BLOCK // 128):
                best = jnp.maximum(best, part[:, t * 128 : (t + 1) * 128])
            return best

        def score(j):
            start = pl.multiple_of(j * KEY_BLOCK, KEY_BLOCK)
            return lax.dot_general(
                rows,
                k_ref[pl.ds(start, KEY_BLOCK), :],
                (((1,), (1,)), ((), ())),
                preferred_element_type=jnp.float32,
            )

        def plain(j, best):
            part = score(j)
            scores[j] = part
            return fold(best, part)

        def masked(j, best):
            part = jnp.where(key_pos + j * KEY_BLOCK <= query_pos, score(j), -1e30)
            scores[j] = part
            return fold(best, part)

        best = jnp.full((GROUP, 128), -1e30, jnp.float32)
        best = lax.fori_loop(0, whole, plain, best)
        best = lax.fori_loop(whole, blocks, masked, best)
        top = jnp.broadcast_to(jnp.max(best, axis=-1, keepdims=True), (GROUP, 128))
        top = jnp.concatenate([top] * (KEY_BLOCK // 128), 1)

        def mix(j, total):
            start = pl.multiple_of(j * KEY_BLOCK, KEY_BLOCK)
            weights = jnp.exp2((scores[j] - top) * gain).astype(jnp.bfloat16)
            return total + jnp.dot(
                weights, wide[pl.ds(start, KEY_BLOCK), :], preferred_element_type=jnp.float32
            )

        total = lax.fori_loop(0, blocks, mix, jnp.zeros((GROUP, 2 * HEAD), jnp.float32))
        normed = (total[:, :HEAD] / total[:, HEAD:]).astype(jnp.bfloat16)
        for h in range(HEADS):
            o_ref[group, :, h * HEAD : (h + 1) * HEAD] = normed[h * HALF : (h + 1) * HALF]


def attention(first, q_pair, key_head, value_head):
    vmem = pl.BlockSpec(memory_space=pltpu.VMEM)
    return pl.pallas_call(
        attention_kernel,
        out_shape=jax.ShapeDtypeStruct((2, HALF, HEADS * HEAD), jnp.bfloat16),
        in_specs=[pl.BlockSpec(memory_space=pltpu.SMEM), vmem, vmem, vmem],
        out_specs=vmem,
        scratch_shapes=[
            pltpu.VMEM((KEYS, 2 * HEAD), jnp.bfloat16),
            pltpu.VMEM((KEYS // KEY_BLOCK, GROUP, KEY_BLOCK), jnp.float32),
        ],
        cost_estimate=pl.CostEstimate(
            flops=4 * 2 * GROUP * KEYS * HEAD, bytes_accessed=3 << 20, transcendentals=2 * GROUP * KEYS
        ),
        name="attend",
    )(first, q_pair, key_head, value_head)


def project_kernel(dest_ref, att_ref, own_ref, other_ref, sign_ref, turn_ref, ones_ref, o_ref):
    signs = (2 * sign_ref[...] - 1).astype(jnp.float32)
    total = None
    for group, weight in ((0, own_ref), (1, other_ref)):
        flat = jnp.dot(att_ref[group], weight[...], preferred_element_type=jnp.float32) * signs
        tall = jnp.concatenate([flat[:, i * 256 : (i + 1) * 256] for i in range(COLS // 256)], 0)
        turned = jnp.dot(
            tall.astype(jnp.bfloat16), turn_ref[...], preferred_element_type=jnp.float32
        ) * (1.0 / math.sqrt(BLOCK))
        squares = jnp.dot(
            (tall * tall).astype(jnp.bfloat16), ones_ref[...], preferred_element_type=jnp.float32
        )
        limit = 2.0 * jnp.sqrt(squares * (1.0 / BLOCK) + 1e-06)
        clipped = jnp.minimum(jnp.maximum(turned, -limit), limit)
        total = clipped if total is None else total + clipped
    for b in range(SUB):
        row, lane = (b // 2) * HALF, (b % 2) * BLOCK
        o_ref[0, b] = total[row : row + HALF, lane : lane + BLOCK].astype(o_ref.dtype)


def project(dests, attended, own, other, signs, turn, ones, kind):
    count = dests.shape[0]
    return pl.pallas_call(
        project_kernel,
        out_shape=jax.ShapeDtypeStruct((count, SUB, HALF, BLOCK), kind),
        grid_spec=pltpu.PrefetchScalarGridSpec(
            num_scalar_prefetch=1,
            grid=(count,),
            in_specs=[
                pl.BlockSpec((2, HALF, HEADS * HEAD), lambda i, d: (0, 0, 0)),
                pl.BlockSpec((HEADS * HEAD, COLS), lambda i, d: (0, d[i])),
                pl.BlockSpec((HEADS * HEAD, COLS), lambda i, d: (0, d[i])),
                pl.BlockSpec((1, COLS), lambda i, d: (0, d[i])),
                pl.BlockSpec((256, 256), lambda i, d: (0, 0)),
                pl.BlockSpec((256, 256), lambda i, d: (0, 0)),
            ],
            out_specs=pl.BlockSpec((1, SUB, HALF, BLOCK), lambda i, d: (i, 0, 0, 0)),
        ),
        cost_estimate=pl.CostEstimate(
            flops=count * 2 * HALF * 1536 * COLS, bytes_accessed=count << 20, transcendentals=0
        ),
        name="project",
    )(dests, attended, own, other, signs, turn, ones)


def pack_kernel(own_ref, up0, up1, down0, down1, o0_ref, o1_ref, square):
    for half, (up, down, out) in enumerate(((up0, down0, o0_ref), (up1, down1, o1_ref))):
        lane = lax.broadcasted_iota(jnp.int32, (HALF, BLOCK), 1)
        columns = jnp.zeros((HALF, BLOCK), jnp.float32)
        for b in range(SUB):
            summed = own_ref[half, b] + (up[b].astype(jnp.float32) + down[b].astype(jnp.float32))
            scale = jnp.max(jnp.abs(summed), axis=-1, keepdims=True) + 1e-06
            out[b * HALF : (b + 1) * HALF, :] = (summed / scale).astype(jnp.bfloat16)
            columns = jnp.where(lane == b, scale, columns)
        square[...] = jnp.zeros((BLOCK, BLOCK), jnp.float32)
        square[:HALF, :] = columns
        rows = square[...].T[:SUB, :]
        upper = rows.astype(jnp.bfloat16).astype(jnp.float32)
        tail = jnp.concatenate([upper, rows - upper, jnp.zeros((8, BLOCK), jnp.float32)], 0)
        out[ROWS:, :] = tail.astype(jnp.bfloat16)


def pack(own, up0, up1, down0, down1):
    vmem = pl.BlockSpec(memory_space=pltpu.VMEM)
    shape = jax.ShapeDtypeStruct((MSG, BLOCK), jnp.bfloat16)
    return pl.pallas_call(
        pack_kernel,
        out_shape=(shape, shape),
        in_specs=[vmem] * 5,
        out_specs=(vmem, vmem),
        scratch_shapes=[pltpu.VMEM((BLOCK, BLOCK), jnp.float32)],
        cost_estimate=pl.CostEstimate(flops=1 << 20, bytes_accessed=1 << 20, transcendentals=0),
        name="pack",
    )(own, up0, up1, down0, down1)


def assemble_kernel(places, index_ref, *refs):
    count = len(places)
    pieces, (out_ref, scale_ref, table, sems) = refs[:count], refs[count:]
    core, chip = index_ref[0], index_ref[1]
    copies = []
    for n, (piece, (swap, offset, half)) in enumerate(zip(pieces, places)):
        side = (1 - core) if swap else core
        place = lax.rem(chip + (offset + CHIPS), CHIPS)
        row = pl.multiple_of(side * HALF, 16)
        for b in range(SUB):
            column = pl.multiple_of(place * CHUNK + half * COLS + b * BLOCK, BLOCK)
            copies.append(
                pltpu.make_async_copy(
                    piece.at[pl.ds(b * HALF, HALF), :],
                    out_ref.at[pl.ds(row, HALF), pl.ds(column, BLOCK)],
                    sems.at[n * SUB + b],
                )
            )
            copies[-1].start()
    for piece, (swap, offset, half) in zip(pieces, places):
        side = (1 - core) if swap else core
        place = lax.rem(chip + (offset + CHIPS), CHIPS)
        tail = piece[ROWS:, :].astype(jnp.float32)
        table[side, place, half * SUB : (half + 1) * SUB, :] = tail[:SUB] + tail[SUB : 2 * SUB]
    zero = jnp.zeros((D // BLOCK, BLOCK), jnp.float32)
    first = jnp.concatenate([table[0].reshape(D // BLOCK, BLOCK), zero], 1)
    second = jnp.concatenate([table[1].reshape(D // BLOCK, BLOCK), zero], 1)
    lane = lax.broadcasted_iota(jnp.int32, first.shape, 1)
    both = jnp.where(lane < HALF, first, pltpu.roll(second, HALF, 1))
    scale_ref[...] = both[:, :TOKENS]
    for copy in copies:
        copy.wait()


def assemble(index, pieces, places):
    vmem = pl.BlockSpec(memory_space=pltpu.VMEM)
    import functools

    return pl.pallas_call(
        functools.partial(assemble_kernel, places),
        out_shape=(
            jax.ShapeDtypeStruct((TOKENS, D), jnp.bfloat16),
            jax.ShapeDtypeStruct((D // BLOCK, TOKENS), jnp.float32),
        ),
        in_specs=[pl.BlockSpec(memory_space=pltpu.SMEM)] + [vmem] * len(pieces),
        out_specs=(pl.BlockSpec(memory_space=pl.ANY), vmem),
        scratch_shapes=[
            pltpu.VMEM((2, CHIPS, 2 * SUB, BLOCK), jnp.float32),
            pltpu.SemaphoreType.DMA((len(pieces) * SUB,)),
        ],
        cost_estimate=pl.CostEstimate(flops=1 << 20, bytes_accessed=8 << 20, transcendentals=0),
        name="assemble",
    )(index, *pieces)


def add(arrived, own):
    return (arrived.astype(jnp.float32) + own.astype(jnp.float32)).astype(jnp.bfloat16)


def local(queries, keys, values, out_weight, signs):
    ctx, tp = lax.axis_index("ctx"), lax.axis_index("tp")
    core, chip = lax.rem(tp, 2), lax.div(tp, 2)

    def send(x, pairs):
        return lax.ppermute(x, "tp", pairs)

    other_weight = send(out_weight, PAIR)
    mine = lax.dynamic_slice_in_dim(queries, core * HALF, HALF, 0)
    theirs = lax.dynamic_slice_in_dim(queries, (1 - core) * HALF, HALF, 0)
    q_pair = jnp.stack([mine, send(theirs, PAIR)])

    key_part = lax.dynamic_slice_in_dim(keys, chip * HEAD, HEAD, 1)
    value_part = lax.dynamic_slice_in_dim(values, chip * HEAD, HEAD, 1)
    half = jnp.where(core == 0, key_part, value_part)
    held = lax.all_gather(half, "ctx", axis=0, tiled=True)
    swapped = send(held, PAIR)
    key_head = jnp.where(core == 0, held, swapped)
    value_head = jnp.where(core == 0, swapped, held)

    first = (ctx * TOKENS + core * HALF).astype(jnp.int32)
    attended = attention(first[None], q_pair, key_head, value_head)

    turn = twice(plus_minus())
    ones = twice(jnp.ones((BLOCK, BLOCK), jnp.bfloat16))
    sign_row = signs[None, :]

    def partials(places, kind=jnp.bfloat16):
        dests = jnp.stack(
            [lax.rem(chip + (offset + CHIPS), CHIPS) * 2 + piece for offset, piece in places]
        ).astype(jnp.int32)
        return project(
            dests, attended, out_weight, other_weight, sign_row, turn, ones, kind
        )

    far = partials([(4, 0), (4, 1)])
    third = partials([(3, 0), (3, 1), (-3, 0), (-3, 1)])
    second = partials([(2, 0), (2, 1), (-2, 0), (-2, 1)])
    near = partials([(1, 0), (1, 1), (-1, 0), (-1, 1)])
    own = partials([(0, 0), (0, 1)], jnp.float32)
    up0, down1 = send(far[0], UP), send(far[1], DOWN)
    up1, down0 = send(third[1], UP), send(third[2], DOWN)
    up0, down1 = send(add(up0, third[0]), UP), send(add(down1, third[3]), DOWN)
    for stage in (second, near):
        up1, down0 = send(add(up1, stage[1]), UP), send(add(down0, stage[2]), DOWN)
        up0, down1 = send(add(up0, stage[0]), UP), send(add(down1, stage[3]), DOWN)

    packed = pack(own, up0, up1, down0, down1)

    pieces, places = [packed[0], packed[1]], [(False, 0, 0), (False, 0, 1)]
    up, down = list(packed), list(packed)
    for hop in range(1, 5):
        for half_index in (0, 1):
            if hop < 4 or half_index == 0:
                up[half_index] = send(up[half_index], UP)
                pieces.append(up[half_index])
                places.append((False, -hop, half_index))
            if hop < 4 or half_index == 0:
                down[1 - half_index] = send(down[1 - half_index], DOWN)
                pieces.append(down[1 - half_index])
                places.append((False, hop, 1 - half_index))
    swapped_pieces = [send(piece, PAIR) for piece in pieces]
    places = places + [(True, offset, h) for _, offset, h in places]
    index = jnp.stack([core, chip]).astype(jnp.int32)
    payload, scales = assemble(index, pieces + swapped_pieces, tuple(places))
    return payload, scales.T


def solution(mesh):
    return jax.shard_map(
        local,
        mesh=mesh,
        in_specs=(P("ctx", "tp"), P("ctx", None), P("ctx", None), P("tp", None), P()),
        out_specs=(P("ctx", None), P("ctx", None)),
        check_vma=False,
    )
```

```python
import functools
import math

import jax
import jax.numpy as jnp
import numpy as np
from jax import lax
from jax.experimental import pallas as pl
from jax.experimental.pallas import tpu as pltpu
from jax.sharding import PartitionSpec as P

D = 8192
HEAD = 128
BLOCK = 128
CHIPS = 8
TOKENS = 224
HALF = TOKENS // 2
HEADS = 4
KEYS = 3584
KEY_BLOCK = 896
CHUNK = D // CHIPS
COLS = 512
SUB = COLS // BLOCK
ROWS = SUB * HALF
MSG = ROWS + 16

UP = [(t, (t + 2) % 16) for t in range(16)]
DOWN = [(t, (t - 2) % 16) for t in range(16)]
PAIR = [(t, t ^ 1) for t in range(16)]


def turn_matrix():
    common = np.arange(BLOCK)[:, None] & np.arange(BLOCK)[None, :]
    parity = np.zeros((BLOCK, BLOCK), np.int64)
    for bit in range(BLOCK.bit_length() - 1):
        parity += (common >> bit) & 1
    return np.kron(np.eye(2), 1 - 2 * (parity % 2)).astype(np.float32)


def spread_matrix():
    row, column = np.arange(BLOCK)[:, None], np.arange(COLS)[None, :]
    return ((row % SUB == column // BLOCK) & (row < 2 * SUB)).astype(np.float32)


def clipped_partial(attended, own, other, signs, turn_ref, spread_ref):
    flat = jnp.concatenate(
        [
            (jnp.dot(attended[group], weight, preferred_element_type=jnp.float32) * signs).astype(
                jnp.bfloat16
            )
            for group, weight in ((0, own), (1, other))
        ],
        0,
    )
    squares = lax.dot_general(
        flat * flat, spread_ref[...], (((1,), (1,)), ((), ())), preferred_element_type=jnp.float32
    )
    limit = 2.0 * jnp.sqrt(squares + BLOCK * 1e-06)
    upper = limit.astype(jnp.bfloat16).astype(jnp.float32)
    lane = lax.broadcasted_iota(jnp.int32, limit.shape, 1)
    limit = jnp.where(lane < SUB, upper, limit - upper).astype(jnp.bfloat16)
    limit = jnp.dot(limit, spread_ref[...], preferred_element_type=jnp.float32)
    tall = jnp.concatenate([flat[:, i * 256 : (i + 1) * 256] for i in range(COLS // 256)], 0)
    turned = jnp.dot(tall, turn_ref[...], preferred_element_type=jnp.float32)
    blocks = []
    for b in range(SUB):
        total = None
        for group in range(2):
            row, lanes = (b // 2) * 2 * HALF + group * HALF, (b % 2) * BLOCK
            bound = limit[group * HALF : (group + 1) * HALF, b * BLOCK : (b + 1) * BLOCK]
            clipped = jnp.minimum(
                jnp.maximum(turned[row : row + HALF, lanes : lanes + BLOCK], -bound), bound
            )
            total = clipped if total is None else total + clipped
        blocks.append(total)
    return blocks


GROUP = HEADS * HALF
LANES = KEY_BLOCK // 128


def heads_kernel(
    place_ref,
    mine_ref,
    theirs_ref,
    held_ref,
    swapped_ref,
    own_hbm,
    other_hbm,
    sign_ref,
    turn_ref,
    spread_ref,
    *refs,
):
    o_refs, (key, wide, scores, attended, own_ref, other_ref, sems) = refs[: 2 * CHIPS], refs[2 * CHIPS :]
    first, core, chip = place_ref[0], place_ref[1], place_ref[2]
    fetches = [
        pltpu.make_async_copy(own_hbm, own_ref, sems.at[0]),
        pltpu.make_async_copy(other_hbm, other_ref, sems.at[1]),
    ]
    for fetch in fetches:
        fetch.start()
    whole = first // KEY_BLOCK
    blocks = (first + HALF - 1) // KEY_BLOCK + 1
    gain = math.log2(math.e) / math.sqrt(HEAD)

    @pl.when(core == 0)
    def _():
        key[...] = held_ref[...]
        wide[:, :HEAD] = swapped_ref[...]

    @pl.when(core != 0)
    def _():
        key[...] = swapped_ref[...]
        wide[:, :HEAD] = held_ref[...]

    wide[:, HEAD:] = jnp.ones((KEYS, HEAD), jnp.bfloat16)
    query_pos = first + lax.rem(
        lax.broadcasted_iota(jnp.int32, (GROUP, 128), 0), HALF
    )
    key_pos = lax.broadcasted_iota(jnp.int32, (GROUP, 128), 1)
    rows = [
        jnp.concatenate([ref[:, h * HEAD : (h + 1) * HEAD] for h in range(HEADS)], 0)
        for ref in (mine_ref, theirs_ref)
    ]

    def score(j, best, masked):
        start = pl.multiple_of(j * KEY_BLOCK, 128)
        result = []
        for group in range(2):
            part = lax.dot_general(
                rows[group],
                key[pl.ds(start, KEY_BLOCK), :],
                (((1,), (1,)), ((), ())),
                preferred_element_type=jnp.float32,
            )
            top = best[group]
            for t in range(LANES):
                piece = part[:, t * 128 : (t + 1) * 128]
                if masked:
                    piece = jnp.where(key_pos <= query_pos - (start + t * 128), piece, -1e30)
                scores[group, j, :, t * 128 : (t + 1) * 128] = piece
                top = jnp.maximum(top, piece)
            result.append(top)
        return tuple(result)

    low = jnp.full((GROUP, 128), -1e30, jnp.float32)
    best = lax.fori_loop(0, whole, lambda j, b: score(j, b, False), (low, low))
    best = lax.fori_loop(whole, blocks, lambda j, b: score(j, b, True), best)
    tops = [jnp.broadcast_to(jnp.max(b, axis=-1, keepdims=True), (GROUP, 128)) for b in best]

    def mix(j, totals):
        start = pl.multiple_of(j * KEY_BLOCK, 128)
        result = []
        for group in range(2):
            weights = jnp.concatenate(
                [
                    jnp.exp2((scores[group, j, :, t * 128 : (t + 1) * 128] - tops[group]) * gain).astype(
                        jnp.bfloat16
                    )
                    for t in range(LANES)
                ],
                1,
            )
            result.append(
                totals[group]
                + jnp.dot(
                    weights, wide[pl.ds(start, KEY_BLOCK), :], preferred_element_type=jnp.float32
                )
            )
        return tuple(result)

    none = jnp.zeros((GROUP, 2 * HEAD), jnp.float32)
    totals = lax.fori_loop(0, blocks, mix, (none, none))
    for group in range(2):
        normed = (totals[group][:, :HEAD] / totals[group][:, HEAD:]).astype(jnp.bfloat16)
        for h in range(HEADS):
            attended[group, :, h * HEAD : (h + 1) * HEAD] = normed[h * HALF : (h + 1) * HALF]

    for fetch in fetches:
        fetch.wait()

    @pl.loop(0, CHIPS)
    def _(step):
        distance = 4 - (step + 1) // 2
        offset = jnp.where(lax.rem(step, 2) == 0, -distance, distance)
        base = lax.rem(chip + offset + CHIPS, CHIPS) * CHUNK
        for half in range(2):
            start = pl.multiple_of(base + half * COLS, COLS)
            signs = (2 * sign_ref[:, pl.ds(start, COLS)] - 1).astype(jnp.float32)
            blocks = clipped_partial(
                attended,
                own_ref[:, pl.ds(start, COLS)],
                other_ref[:, pl.ds(start, COLS)],
                signs,
                turn_ref,
                spread_ref,
            )
            for n in range(CHIPS):

                @pl.when(step == n)
                def _(o_ref=o_refs[2 * n + half], blocks=blocks):
                    for b in range(SUB):
                        o_ref[b * HALF : (b + 1) * HALF, :] = blocks[b].astype(o_ref.dtype)


VMEM = pl.BlockSpec(memory_space=pltpu.VMEM)
SMEM = pl.BlockSpec(memory_space=pltpu.SMEM)
ANY = pl.BlockSpec(memory_space=pl.ANY)


HBM = pl.BlockSpec(memory_space=pltpu.HBM)


def heads(place, mine, theirs, held, swapped, own, other, signs, turn, spread):
    half = jax.ShapeDtypeStruct((ROWS, BLOCK), jnp.bfloat16)
    full = jax.ShapeDtypeStruct((ROWS, BLOCK), jnp.float32)
    return pl.pallas_call(
        heads_kernel,
        out_shape=(half,) * (2 * CHIPS - 2) + (full,) * 2,
        in_specs=[SMEM, VMEM, VMEM, VMEM, VMEM, HBM, HBM, VMEM, VMEM, VMEM],
        out_specs=(VMEM,) * (2 * CHIPS),
        scratch_shapes=[
            pltpu.VMEM((KEYS, HEAD), jnp.bfloat16),
            pltpu.VMEM((KEYS, 2 * HEAD), jnp.bfloat16),
            pltpu.VMEM((2, KEYS // KEY_BLOCK, GROUP, KEY_BLOCK), jnp.float32),
            pltpu.VMEM((2, HALF, HEADS * HEAD), jnp.bfloat16),
            pltpu.VMEM((HEADS * HEAD, D), jnp.bfloat16),
            pltpu.VMEM((HEADS * HEAD, D), jnp.bfloat16),
            pltpu.SemaphoreType.DMA((2,)),
        ],
        compiler_params=pltpu.CompilerParams(vmem_limit_bytes=48 << 20),
        cost_estimate=pl.CostEstimate(
            flops=8 * GROUP * KEYS * HEAD + 2 * HALF * 1536 * D,
            bytes_accessed=20 << 20,
            transcendentals=2 * GROUP * KEYS,
        ),
        name="heads",
    )(place, mine, theirs, held, swapped, own, other, signs, turn, spread)


def pack_kernel(own0, own1, up0, up1, down0, down1, o0_ref, o1_ref, square):
    for own, up, down, out in ((own0, up0, down0, o0_ref), (own1, up1, down1, o1_ref)):
        lane = lax.broadcasted_iota(jnp.int32, (HALF, BLOCK), 1)
        columns = jnp.zeros((HALF, BLOCK), jnp.float32)
        for b in range(SUB):
            rows = slice(b * HALF, (b + 1) * HALF)
            came = up[rows, :].astype(jnp.float32) + down[rows, :].astype(jnp.float32)
            summed = (own[rows, :] + came) * (1.0 / math.sqrt(BLOCK))
            scale = jnp.max(jnp.abs(summed), axis=-1, keepdims=True) + 1e-06
            out[rows, :] = (summed / scale).astype(jnp.bfloat16)
            columns = jnp.where(lane == b, scale, columns)
        square[...] = jnp.zeros((BLOCK, BLOCK), jnp.float32)
        square[:HALF, :] = columns
        turned = square[...].T[:SUB, :]
        upper = turned.astype(jnp.bfloat16).astype(jnp.float32)
        tail = jnp.concatenate([upper, turned - upper, jnp.zeros((8, BLOCK), jnp.float32)], 0)
        out[ROWS:, :] = tail.astype(jnp.bfloat16)


def pack(own, up, down):
    shape = jax.ShapeDtypeStruct((MSG, BLOCK), jnp.bfloat16)
    return pl.pallas_call(
        pack_kernel,
        out_shape=(shape, shape),
        in_specs=[VMEM] * 6,
        out_specs=(VMEM, VMEM),
        scratch_shapes=[pltpu.VMEM((BLOCK, BLOCK), jnp.float32)],
        compiler_params=pltpu.CompilerParams(vmem_limit_bytes=8 << 20),
        cost_estimate=pl.CostEstimate(flops=1 << 20, bytes_accessed=1 << 20, transcendentals=0),
        name="pack",
    )(*own, *up, *down)


def assemble_kernel(places, fresh, last, index_ref, *refs):
    count = 1 + max(place[0] for place in places)
    arrays, refs = refs[:count], refs[count:]
    if fresh:
        out_ref, table, tails, sems, tail_sems = refs
    else:
        _, old_table, out_ref, table, tails, sems, tail_sems = refs[:7]
        if last:
            _, _, out_ref, scale_ref, table, tails, sems, tail_sems = refs
        table[...] = old_table[...]
    core, chip = index_ref[0], index_ref[1]

    def spot(swap, offset):
        side = (1 - core) if swap else core
        return side, lax.rem(chip + offset + CHIPS, CHIPS)

    copies, tail_copies = [], []
    for n, (array, row, swap, offset, half) in enumerate(places):
        tail_copies.append(
            pltpu.make_async_copy(
                arrays[array].at[pl.ds(row + ROWS, 16), :], tails.at[n], tail_sems.at[n]
            )
        )
        tail_copies[-1].start()
    for n, (array, row, swap, offset, half) in enumerate(places):
        side, place = spot(swap, offset)
        for b in range(SUB):
            column = pl.multiple_of(place * CHUNK + half * COLS + b * BLOCK, BLOCK)
            copies.append(
                pltpu.make_async_copy(
                    arrays[array].at[pl.ds(row + b * HALF, HALF), :],
                    out_ref.at[pl.ds(pl.multiple_of(side * HALF, 16), HALF), pl.ds(column, BLOCK)],
                    sems.at[n * SUB + b],
                )
            )
            copies[-1].start()
    for n, (array, row, swap, offset, half) in enumerate(places):
        tail_copies[n].wait()
        side, place = spot(swap, offset)
        tail = tails[n].astype(jnp.float32)
        table[side, place, half * SUB : (half + 1) * SUB, :] = tail[:SUB] + tail[SUB : 2 * SUB]
    if last:
        zero = jnp.zeros((D // BLOCK, BLOCK), jnp.float32)
        first = jnp.concatenate([table[0].reshape(D // BLOCK, BLOCK), zero], 1)
        second = jnp.concatenate([table[1].reshape(D // BLOCK, BLOCK), zero], 1)
        lane = lax.broadcasted_iota(jnp.int32, first.shape, 1)
        both = jnp.where(lane < HALF, first, pltpu.roll(second, HALF, 1))
        scale_ref[...] = both[:, :TOKENS]
    for copy in copies:
        copy.wait()


def assemble(index, arrays, places, before, last):
    table_shape = (2, CHIPS, 2 * SUB, BLOCK)
    out_shape = [jax.ShapeDtypeStruct((TOKENS, D), jnp.bfloat16)]
    out_shape.append(
        jax.ShapeDtypeStruct((D // BLOCK, TOKENS) if last else table_shape, jnp.float32)
    )
    scratch = [pltpu.VMEM(table_shape, jnp.float32)] if last else []
    fresh = before is None
    return pl.pallas_call(
        functools.partial(assemble_kernel, places, fresh, last),
        out_shape=tuple(out_shape),
        in_specs=[SMEM] + [ANY] * len(arrays) + ([] if fresh else [ANY, VMEM]),
        out_specs=(ANY, VMEM),
        scratch_shapes=scratch
        + [
            pltpu.VMEM((len(places), 16, BLOCK), jnp.bfloat16),
            pltpu.SemaphoreType.DMA((len(places) * SUB,)),
            pltpu.SemaphoreType.DMA((len(places),)),
        ],
        input_output_aliases={} if fresh else {len(arrays) + 1: 0},
        compiler_params=pltpu.CompilerParams(vmem_limit_bytes=4 << 20),
        cost_estimate=pl.CostEstimate(flops=1 << 20, bytes_accessed=4 << 20, transcendentals=0),
        name="assemble",
    )(index, *arrays, *([] if fresh else before))


def add(arrived, own):
    return (arrived.astype(jnp.float32) + own.astype(jnp.float32)).astype(jnp.bfloat16)


def send(x, pairs):
    return lax.ppermute(x, "tp", pairs)


EARLY = 12


def local(queries, keys, values, out_weight, signs):
    ctx, tp = lax.axis_index("ctx"), lax.axis_index("tp")
    core, chip = tp & 1, tp >> 1

    mine = lax.dynamic_slice_in_dim(queries, core * HALF, HALF, 0)
    theirs = send(lax.dynamic_slice_in_dim(queries, (1 - core) * HALF, HALF, 0), PAIR)

    key_part = lax.dynamic_slice_in_dim(keys, chip * HEAD, HEAD, 1)
    value_part = lax.dynamic_slice_in_dim(values, chip * HEAD, HEAD, 1)
    half = jnp.where(core == 0, key_part, value_part)
    weight, half, theirs, mine = lax.optimization_barrier((out_weight, half, theirs, mine))
    other_weight = send(weight, PAIR)
    held = lax.all_gather(half, "ctx", axis=0, tiled=True)
    swapped = send(held, PAIR)

    at = jnp.stack([ctx * TOKENS + core * HALF, core, chip]).astype(jnp.int32)
    index = jnp.stack([core, chip]).astype(jnp.int32)
    turn = jnp.asarray(turn_matrix(), jnp.bfloat16)
    spread = jnp.asarray(spread_matrix(), jnp.bfloat16)
    parts = heads(
        at, mine, theirs, held, swapped, out_weight, other_weight, signs[None, :], turn, spread
    )

    up, down = [send(parts[0], UP), None], [None, send(parts[1], DOWN)]
    up[1], down[0] = send(parts[3], UP), send(parts[4], DOWN)
    up[0], down[1] = send(add(up[0], parts[2]), UP), send(add(down[1], parts[5]), DOWN)
    for near in (6, 10):
        up[1], down[0] = send(add(up[1], parts[near + 1]), UP), send(add(down[0], parts[near + 2]), DOWN)
        up[0], down[1] = send(add(up[0], parts[near]), UP), send(add(down[1], parts[near + 3]), DOWN)

    packed = pack(parts[14:], up, down)

    pieces, spots = list(packed), [(0, 0), (0, 1)]
    up, down = list(packed), list(packed)
    for hop in range(1, 5):
        for h in (0, 1):
            if hop < 4 or h == 0:
                up[h], down[1 - h] = send(up[h], UP), send(down[1 - h], DOWN)
                pieces += [up[h], down[1 - h]]
                spots += [(-hop, h), (hop, 1 - h)]
    early = send(jnp.concatenate(pieces[:EARLY], 0), PAIR)
    late = [send(piece, PAIR) for piece in pieces[EARLY:]]

    def rows(swap, a, b, packed_rows=False):
        return tuple(
            (0 if packed_rows else n - a, (n - a) * MSG if packed_rows else 0, swap, *spots[n])
            for n in range(a, b)
        )

    first = assemble(index, pieces[:EARLY], rows(False, 0, EARLY), None, False)
    second = assemble(index, [early], rows(True, 0, EARLY, True), first, False)
    count = len(pieces) - EARLY
    tail = rows(False, EARLY, len(pieces)) + tuple(
        (n + count, row, True, *spot) for n, row, _, *spot in rows(False, EARLY, len(pieces))
    )
    payload, scales = assemble(index, pieces[EARLY:] + late, tail, second, True)
    return payload, scales.T


def solution(mesh):
    return jax.shard_map(
        local,
        mesh=mesh,
        in_specs=(P("ctx", "tp"), P("ctx", None), P("ctx", None), P("tp", None), P()),
        out_specs=(P("ctx", None), P("ctx", None)),
        check_vma=False,
    )
```

```python
import functools
import math

import jax
import jax.numpy as jnp
import numpy as np
from jax import lax
from jax.experimental import pallas as pl
from jax.experimental.pallas import tpu as pltpu
from jax.sharding import PartitionSpec as P

D = 8192
HEAD = 128
BLOCK = 128
CHIPS = 8
TOKENS = 224
HEADS = 4
WIDTH = HEADS * HEAD
KEYS = 3584
KEY_BLOCK = 896
CHUNK = D // CHIPS
SHARE = CHUNK // 2
COLS = SHARE // 2
SUB = COLS // BLOCK
ROWS = SUB * TOKENS
MSG = ROWS + 16

UP = [(t, (t + 2) % 16) for t in range(16)]
DOWN = [(t, (t - 2) % 16) for t in range(16)]
PAIR = [(t, t ^ 1) for t in range(16)]


def turn_matrix():
    common = np.arange(BLOCK)[:, None] & np.arange(BLOCK)[None, :]
    parity = np.zeros((BLOCK, BLOCK), np.int64)
    for bit in range(BLOCK.bit_length() - 1):
        parity += (common >> bit) & 1
    return np.kron(np.eye(2), 1 - 2 * (parity % 2)).astype(np.float32)


def spread_matrix():
    row, column = np.arange(BLOCK)[:, None], np.arange(COLS)[None, :]
    return ((row % SUB == column // BLOCK) & (row < 2 * SUB)).astype(np.float32)


def clipped_partial(pairs, signs, turn_ref, spread_ref):
    flat = jnp.concatenate(
        [
            (jnp.dot(rows, weight, preferred_element_type=jnp.float32) * signs).astype(jnp.bfloat16)
            for rows, weight in pairs
        ],
        0,
    )
    squares = lax.dot_general(
        flat * flat, spread_ref[...], (((1,), (1,)), ((), ())), preferred_element_type=jnp.float32
    )
    limit = 2.0 * jnp.sqrt(squares + BLOCK * 1e-06)
    upper = limit.astype(jnp.bfloat16).astype(jnp.float32)
    lane = lax.broadcasted_iota(jnp.int32, limit.shape, 1)
    limit = jnp.where(lane < SUB, upper, limit - upper).astype(jnp.bfloat16)
    limit = jnp.dot(limit, spread_ref[...], preferred_element_type=jnp.float32)
    turned = jnp.dot(flat, turn_ref[...], preferred_element_type=jnp.float32)
    clipped = jnp.minimum(jnp.maximum(turned, -limit), limit)
    return clipped[:TOKENS] + clipped[TOKENS:]


GROUP = HEADS // 2 * TOKENS
LANES = KEY_BLOCK // 128


def attention_kernel(place_ref, query_ref, held_ref, swapped_ref, o_ref, key, wide, scores):
    first, core = place_ref[0], place_ref[1]
    whole = first // KEY_BLOCK
    blocks = (first + TOKENS - 1) // KEY_BLOCK + 1
    gain = math.log2(math.e) / math.sqrt(HEAD)

    @pl.when(core == 0)
    def _():
        key[...] = held_ref[...]
        wide[:, :HEAD] = swapped_ref[...]

    @pl.when(core != 0)
    def _():
        key[...] = swapped_ref[...]
        wide[:, :HEAD] = held_ref[...]

    wide[:, HEAD:] = jnp.ones((KEYS, HEAD), jnp.bfloat16)
    query_pos = first + lax.rem(
        lax.broadcasted_iota(jnp.int32, (GROUP, 128), 0), TOKENS
    )
    key_pos = lax.broadcasted_iota(jnp.int32, (GROUP, 128), 1)
    rows = [
        jnp.concatenate([query_ref[:, h * HEAD : (h + 1) * HEAD] for h in (2 * g, 2 * g + 1)], 0)
        for g in range(2)
    ]

    def score(j, best, masked):
        start = pl.multiple_of(j * KEY_BLOCK, 128)
        result = []
        for group in range(2):
            part = lax.dot_general(
                rows[group],
                key[pl.ds(start, KEY_BLOCK), :],
                (((1,), (1,)), ((), ())),
                preferred_element_type=jnp.float32,
            )
            top = best[group]
            for t in range(LANES):
                piece = part[:, t * 128 : (t + 1) * 128]
                if masked:
                    piece = jnp.where(key_pos <= query_pos - (start + t * 128), piece, -1e30)
                scores[group, j, :, t * 128 : (t + 1) * 128] = piece
                top = jnp.maximum(top, piece)
            result.append(top)
        return tuple(result)

    low = jnp.full((GROUP, 128), -1e30, jnp.float32)
    best = lax.fori_loop(0, whole, lambda j, b: score(j, b, False), (low, low))
    best = lax.fori_loop(whole, blocks, lambda j, b: score(j, b, True), best)
    tops = [jnp.broadcast_to(jnp.max(b, axis=-1, keepdims=True), (GROUP, 128)) for b in best]

    def mix(j, totals):
        start = pl.multiple_of(j * KEY_BLOCK, 128)
        result = []
        for group in range(2):
            weights = jnp.concatenate(
                [
                    jnp.exp2((scores[group, j, :, t * 128 : (t + 1) * 128] - tops[group]) * gain).astype(
                        jnp.bfloat16
                    )
                    for t in range(LANES)
                ],
                1,
            )
            result.append(
                totals[group]
                + jnp.dot(
                    weights, wide[pl.ds(start, KEY_BLOCK), :], preferred_element_type=jnp.float32
                )
            )
        return tuple(result)

    none = jnp.zeros((GROUP, 2 * HEAD), jnp.float32)
    totals = lax.fori_loop(0, blocks, mix, (none, none))
    for group in range(2):
        normed = (totals[group][:, :HEAD] / totals[group][:, HEAD:]).astype(jnp.bfloat16)
        for h in range(2):
            column = (2 * group + h) * HEAD
            o_ref[:, column : column + HEAD] = normed[h * TOKENS : (h + 1) * TOKENS]


VMEM = pl.BlockSpec(memory_space=pltpu.VMEM)
SMEM = pl.BlockSpec(memory_space=pltpu.SMEM)
ANY = pl.BlockSpec(memory_space=pl.ANY)


HBM = pl.BlockSpec(memory_space=pltpu.HBM)


def attention(place, queries, held, swapped):
    return pl.pallas_call(
        attention_kernel,
        out_shape=jax.ShapeDtypeStruct((TOKENS, WIDTH), jnp.bfloat16),
        in_specs=[SMEM, VMEM, VMEM, VMEM],
        out_specs=VMEM,
        scratch_shapes=[
            pltpu.VMEM((KEYS, HEAD), jnp.bfloat16),
            pltpu.VMEM((KEYS, 2 * HEAD), jnp.bfloat16),
            pltpu.VMEM((2, KEYS // KEY_BLOCK, GROUP, KEY_BLOCK), jnp.float32),
        ],
        compiler_params=pltpu.CompilerParams(vmem_limit_bytes=30 << 20),
        cost_estimate=pl.CostEstimate(
            flops=8 * GROUP * KEYS * HEAD, bytes_accessed=3 << 20, transcendentals=2 * GROUP * KEYS
        ),
        name="attend",
    )(place, queries, held, swapped)


def project_kernel(
    place_ref, mine_ref, theirs_ref, own_hbm, other_hbm, sign_ref, turn_ref, spread_ref, *refs
):
    o_refs, (own, other, sems) = refs[: 2 * CHIPS], refs[2 * CHIPS :]
    core, chip = place_ref[1], place_ref[2]

    def column(step):
        distance = 4 - (step + 1) // 2
        offset = jnp.where(lax.rem(step, 2) == 0, -distance, distance)
        return lax.rem(chip + offset + CHIPS, CHIPS) * CHUNK + core * SHARE

    def fetches(step):
        start = pl.multiple_of(column(step), SHARE)
        return [
            pltpu.make_async_copy(
                source.at[:, pl.ds(start, SHARE)], target.at[step], sems.at[n, step]
            )
            for n, (source, target) in enumerate(((own_hbm, own), (other_hbm, other)))
        ]

    for step in range(CHIPS):
        for fetch in fetches(jnp.int32(step)):
            fetch.start()

    @pl.loop(0, CHIPS)
    def _(step):
        for fetch in fetches(step):
            fetch.wait()
        start = pl.multiple_of(column(step), SHARE)
        for half in range(2):
            columns = slice(half * COLS, (half + 1) * COLS)
            signs = (2 * sign_ref[:, pl.ds(start + half * COLS, COLS)] - 1).astype(jnp.float32)
            total = clipped_partial(
                ((mine_ref[...], own[step, :, columns]), (theirs_ref[...], other[step, :, columns])),
                signs,
                turn_ref,
                spread_ref,
            )
            for n in range(CHIPS):

                @pl.when(step == n)
                def _(o_ref=o_refs[2 * n + half], total=total):
                    for b in range(SUB):
                        piece = total[:, b * BLOCK : (b + 1) * BLOCK]
                        o_ref[b * TOKENS : (b + 1) * TOKENS, :] = piece.astype(o_ref.dtype)


def project(place, mine, theirs, own, other, signs, turn, spread):
    half = jax.ShapeDtypeStruct((ROWS, BLOCK), jnp.bfloat16)
    full = jax.ShapeDtypeStruct((ROWS, BLOCK), jnp.float32)
    return pl.pallas_call(
        project_kernel,
        out_shape=(half,) * (2 * CHIPS - 2) + (full,) * 2,
        in_specs=[SMEM, VMEM, VMEM, HBM, HBM, VMEM, VMEM, VMEM],
        out_specs=(VMEM,) * (2 * CHIPS),
        scratch_shapes=[
            pltpu.VMEM((CHIPS, WIDTH, SHARE), jnp.bfloat16),
            pltpu.VMEM((CHIPS, WIDTH, SHARE), jnp.bfloat16),
            pltpu.SemaphoreType.DMA((2, CHIPS)),
        ],
        compiler_params=pltpu.CompilerParams(vmem_limit_bytes=50 << 20),
        cost_estimate=pl.CostEstimate(
            flops=2 * TOKENS * 1280 * D // 2, bytes_accessed=10 << 20, transcendentals=0
        ),
        name="project",
    )(place, mine, theirs, own, other, signs, turn, spread)


def pack_kernel(own0, own1, up0, up1, down0, down1, o0_ref, o1_ref, square):
    for own, up, down, out in ((own0, up0, down0, o0_ref), (own1, up1, down1, o1_ref)):
        lane = lax.broadcasted_iota(jnp.int32, (TOKENS, BLOCK), 1)
        columns = jnp.zeros((TOKENS, BLOCK), jnp.float32)
        for b in range(SUB):
            rows = slice(b * TOKENS, (b + 1) * TOKENS)
            came = up[rows, :].astype(jnp.float32) + down[rows, :].astype(jnp.float32)
            summed = (own[rows, :] + came) * (1.0 / math.sqrt(BLOCK))
            scale = jnp.max(jnp.abs(summed), axis=-1, keepdims=True) + 1e-06
            out[rows, :] = (summed / scale).astype(jnp.bfloat16)
            columns = jnp.where(lane == b, scale, columns)
        square[...] = jnp.zeros((2 * BLOCK, BLOCK), jnp.float32)
        square[:TOKENS, :] = columns
        turned = jnp.concatenate(
            [square[:BLOCK, :].T[:SUB, :], square[BLOCK:, :].T[:SUB, :]], 0
        )
        upper = turned.astype(jnp.bfloat16).astype(jnp.float32)
        tail = jnp.concatenate([upper, turned - upper, jnp.zeros((8, BLOCK), jnp.float32)], 0)
        out[ROWS:, :] = tail.astype(jnp.bfloat16)


def pack(own, up, down):
    shape = jax.ShapeDtypeStruct((MSG, BLOCK), jnp.bfloat16)
    return pl.pallas_call(
        pack_kernel,
        out_shape=(shape, shape),
        in_specs=[VMEM] * 6,
        out_specs=(VMEM, VMEM),
        scratch_shapes=[pltpu.VMEM((2 * BLOCK, BLOCK), jnp.float32)],
        compiler_params=pltpu.CompilerParams(vmem_limit_bytes=8 << 20),
        cost_estimate=pl.CostEstimate(flops=1 << 20, bytes_accessed=1 << 20, transcendentals=0),
        name="pack",
    )(*own, *up, *down)


def assemble_kernel(places, fresh, last, index_ref, *refs):
    count = 1 + max(place[0] for place in places)
    arrays, refs = refs[:count], refs[count:]
    if fresh:
        out_ref, table, tails, sems, tail_sems = refs
    else:
        _, old_table, out_ref, table, tails, sems, tail_sems = refs[:7]
        if last:
            _, _, out_ref, scale_ref, table, tails, sems, tail_sems = refs
        table[...] = old_table[...]
    core, chip = index_ref[0], index_ref[1]

    def spot(swap, offset):
        side = (1 - core) if swap else core
        return side, lax.rem(chip + offset + CHIPS, CHIPS)

    copies, tail_copies = [], []
    for n, (array, row, swap, offset, half) in enumerate(places):
        tail_copies.append(
            pltpu.make_async_copy(
                arrays[array].at[pl.ds(row + ROWS, 16), :], tails.at[n], tail_sems.at[n]
            )
        )
        tail_copies[-1].start()
    for n, (array, row, swap, offset, half) in enumerate(places):
        side, place = spot(swap, offset)
        for b in range(SUB):
            column = pl.multiple_of(place * CHUNK + side * SHARE + half * COLS + b * BLOCK, BLOCK)
            copies.append(
                pltpu.make_async_copy(
                    arrays[array].at[pl.ds(row + b * TOKENS, TOKENS), :],
                    out_ref.at[:, pl.ds(column, BLOCK)],
                    sems.at[n * SUB + b],
                )
            )
            copies[-1].start()
    for n, (array, row, swap, offset, half) in enumerate(places):
        tail_copies[n].wait()
        side, place = spot(swap, offset)
        tail = tails[n].astype(jnp.float32)
        tail = tail[: 2 * SUB] + tail[2 * SUB : 4 * SUB]
        for t in range(2):
            table[place, side, half * SUB : (half + 1) * SUB, t * BLOCK : (t + 1) * BLOCK] = tail[
                t * SUB : (t + 1) * SUB
            ]
    if last:
        for place in range(CHIPS):
            for side in range(2):
                row = (2 * place + side) * 2 * SUB
                scale_ref[row : row + 2 * SUB, :] = table[place, side][:, :TOKENS]
    for copy in copies:
        copy.wait()


def assemble(index, arrays, places, before, last):
    table_shape = (CHIPS, 2, 2 * SUB, 2 * BLOCK)
    out_shape = [jax.ShapeDtypeStruct((TOKENS, D), jnp.bfloat16)]
    out_shape.append(
        jax.ShapeDtypeStruct((D // BLOCK, TOKENS) if last else table_shape, jnp.float32)
    )
    scratch = [pltpu.VMEM(table_shape, jnp.float32)] if last else []
    fresh = before is None
    return pl.pallas_call(
        functools.partial(assemble_kernel, places, fresh, last),
        out_shape=tuple(out_shape),
        in_specs=[SMEM] + [ANY] * len(arrays) + ([] if fresh else [ANY, VMEM]),
        out_specs=(ANY, VMEM),
        scratch_shapes=scratch
        + [
            pltpu.VMEM((len(places), 16, BLOCK), jnp.bfloat16),
            pltpu.SemaphoreType.DMA((len(places) * SUB,)),
            pltpu.SemaphoreType.DMA((len(places),)),
        ],
        input_output_aliases={} if fresh else {len(arrays) + 1: 0},
        compiler_params=pltpu.CompilerParams(vmem_limit_bytes=4 << 20),
        cost_estimate=pl.CostEstimate(flops=1 << 20, bytes_accessed=4 << 20, transcendentals=0),
        name="assemble",
    )(index, *arrays, *([] if fresh else before))


def add(arrived, own):
    return (arrived.astype(jnp.float32) + own.astype(jnp.float32)).astype(jnp.bfloat16)


def send(x, pairs):
    return lax.ppermute(x, "tp", pairs)


EARLY = 12


def local(queries, keys, values, out_weight, signs):
    ctx, tp = lax.axis_index("ctx"), lax.axis_index("tp")
    core, chip = tp & 1, tp >> 1

    other_weight = send(out_weight, PAIR)
    key_part = lax.dynamic_slice_in_dim(keys, chip * HEAD, HEAD, 1)
    value_part = lax.dynamic_slice_in_dim(values, chip * HEAD, HEAD, 1)
    held = lax.all_gather(jnp.where(core == 0, key_part, value_part), "ctx", axis=0, tiled=True)
    swapped = send(held, PAIR)

    place = jnp.stack([ctx * TOKENS, core, chip]).astype(jnp.int32)
    index = jnp.stack([core, chip]).astype(jnp.int32)
    turn = jnp.asarray(turn_matrix(), jnp.bfloat16)
    spread = jnp.asarray(spread_matrix(), jnp.bfloat16)
    attended = attention(place, queries, held, swapped)
    parts = project(
        place,
        attended,
        send(attended, PAIR),
        out_weight,
        other_weight,
        signs[None, :],
        turn,
        spread,
    )

    a = send(parts[0], UP), send(parts[1], DOWN)
    b = send(parts[3], UP), send(parts[4], DOWN)
    a = lax.optimization_barrier(a)
    a = send(add(a[0], parts[2]), UP), send(add(a[1], parts[5]), DOWN)
    for near in (6, 10):
        b = lax.optimization_barrier(b)
        b = send(add(b[0], parts[near + 1]), UP), send(add(b[1], parts[near + 2]), DOWN)
        a = lax.optimization_barrier(a)
        a = send(add(a[0], parts[near]), UP), send(add(a[1], parts[near + 3]), DOWN)
    packed = pack(parts[14:], (a[0], b[0]), (b[1], a[1]))

    pieces, spots = list(packed), [(0, 0), (0, 1)]
    chains = [(packed[0], packed[1]), (packed[1], packed[0])]
    for step in range(7):
        h, hop = step % 2, step // 2 + 1
        up, down = lax.optimization_barrier(chains[h])
        chains[h] = send(up, UP), send(down, DOWN)
        pieces += chains[h]
        spots += [(-hop, h), (hop, 1 - h)]

    def rows(swap, a, b, joined):
        return tuple(
            (0 if joined else n - a, (n - a) * MSG if joined else 0, swap, *spots[n])
            for n in range(a, b)
        )

    first = assemble(index, pieces[:EARLY], rows(False, 0, EARLY, False), None, False)
    early, first, pieces[EARLY : EARLY + 2] = lax.optimization_barrier(
        (jnp.concatenate(pieces[:EARLY], 0), first, pieces[EARLY : EARLY + 2])
    )
    early = send(early, PAIR)
    rest = jnp.concatenate(pieces[EARLY:], 0)
    late = send(rest, PAIR)
    second = assemble(index, [early], rows(True, 0, EARLY, True), first, False)
    count = len(pieces) - EARLY
    tail = rows(False, EARLY, EARLY + count, True) + tuple(
        (1, *where[1:]) for where in rows(True, EARLY, EARLY + count, True)
    )
    payload, scales = assemble(index, [rest, late], tail, second, True)
    return payload, scales.T


def solution(mesh):
    return jax.shard_map(
        local,
        mesh=mesh,
        in_specs=(P("ctx", "tp"), P("ctx", None), P("ctx", None), P("tp", None), P()),
        out_specs=(P("ctx", None), P("ctx", None)),
        check_vma=False,
    )
```

```python
import functools
import math

import jax
import jax.numpy as jnp
import numpy as np
from jax import lax
from jax.experimental import pallas as pl
from jax.experimental.pallas import tpu as pltpu
from jax.sharding import PartitionSpec as P


D = 8192
HEAD = 128
BLOCK = 128
CHIPS = 8
TOKENS = 224
HEADS = 4
WIDTH = HEADS * HEAD
KEYS = 3584
KEY_BLOCK = 896
CHUNK = D // CHIPS
SHARE = CHUNK // 2
COLS = SHARE // 2
SUB = COLS // BLOCK
ROWS = SUB * TOKENS
MSG = ROWS + 16

UP = [(t, (t + 2) % 16) for t in range(16)]
DOWN = [(t, (t - 2) % 16) for t in range(16)]
PAIR = [(t, t ^ 1) for t in range(16)]

SIDE = 4


def torus_pairs(axis_of_core, step):
    pairs = []
    for c in range(SIDE * SIDE):
        for t in range(16):
            y, x = divmod(c, SIDE)
            if axis_of_core[t % 2] == "x":
                x = (x + step) % SIDE
            else:
                y = (y + step) % SIDE
            pairs.append((c * 16 + t, (y * SIDE + x) * 16 + t))
    return pairs


FIRST = torus_pairs("xy", 1), torus_pairs("xy", -1)
SECOND = torus_pairs("yx", 1), torus_pairs("yx", -1)


def turn_matrix():
    common = np.arange(BLOCK)[:, None] & np.arange(BLOCK)[None, :]
    parity = np.zeros((BLOCK, BLOCK), np.int64)
    for bit in range(BLOCK.bit_length() - 1):
        parity += (common >> bit) & 1
    return np.kron(np.eye(2), 1 - 2 * (parity % 2)).astype(np.float32)


def spread_matrix():
    row, column = np.arange(BLOCK)[:, None], np.arange(COLS)[None, :]
    return ((row % SUB == column // BLOCK) & (row < 2 * SUB)).astype(np.float32)


def clipped_partial(pairs, signs, turn_ref, spread_ref):
    flat = jnp.concatenate(
        [
            (jnp.dot(rows, weight, preferred_element_type=jnp.float32) * signs).astype(jnp.bfloat16)
            for rows, weight in pairs
        ],
        0,
    )
    squares = lax.dot_general(
        flat * flat, spread_ref[...], (((1,), (1,)), ((), ())), preferred_element_type=jnp.float32
    )
    limit = 2.0 * jnp.sqrt(squares + BLOCK * 1e-06)
    upper = limit.astype(jnp.bfloat16).astype(jnp.float32)
    lane = lax.broadcasted_iota(jnp.int32, limit.shape, 1)
    limit = jnp.where(lane < SUB, upper, limit - upper).astype(jnp.bfloat16)
    limit = jnp.dot(limit, spread_ref[...], preferred_element_type=jnp.float32)
    turned = jnp.dot(flat, turn_ref[...], preferred_element_type=jnp.float32)
    clipped = jnp.minimum(jnp.maximum(turned, -limit), limit)
    return clipped[:TOKENS] + clipped[TOKENS:]


GROUP = HEADS // 2 * TOKENS
LANES = KEY_BLOCK // 128


def attention_kernel(place_ref, query_hbm, held_ref, swapped_ref, o_ref, key, wide, scores, query_ref, sem):
    first, core, y, x = place_ref[0], place_ref[1], place_ref[3], place_ref[4]
    fetch = pltpu.make_async_copy(query_hbm, query_ref, sem)
    fetch.start()
    blocks = (first + TOKENS - 1) // KEY_BLOCK + 1
    gain = math.log2(math.e) / math.sqrt(HEAD)

    def sort(keys_ref, values_ref):
        @pl.loop(0, SIDE * SIDE)
        def _(n):
            far, near = (
                jnp.where(i == 1, SIDE - 1, jnp.maximum(i - 1, 0)) for i in (n // SIDE, lax.rem(n, SIDE))
            )
            block = pl.multiple_of(n * TOKENS, 32)
            row, column = lax.rem(y + far, SIDE), lax.rem(x + near, SIDE)
            start = pl.multiple_of((row * SIDE + column) * TOKENS, 32)
            key[pl.ds(start, TOKENS), :] = keys_ref[pl.ds(block, TOKENS), :]
            row, column = lax.rem(y + near, SIDE), lax.rem(x + far, SIDE)
            start = pl.multiple_of((row * SIDE + column) * TOKENS, 32)
            wide[pl.ds(start, TOKENS), :HEAD] = values_ref[pl.ds(block, TOKENS), :]

    @pl.when(core == 0)
    def _():
        sort(held_ref, swapped_ref)

    @pl.when(core != 0)
    def _():
        sort(swapped_ref, held_ref)

    wide[:, HEAD:] = jnp.ones((KEYS, HEAD), jnp.bfloat16)
    fetch.wait()
    query_pos = first + lax.rem(
        lax.broadcasted_iota(jnp.int32, (GROUP, 128), 0), TOKENS
    )
    key_pos = lax.broadcasted_iota(jnp.int32, (GROUP, 128), 1)
    rows = [
        jnp.concatenate([query_ref[:, h * HEAD : (h + 1) * HEAD] for h in (2 * g, 2 * g + 1)], 0)
        for g in range(2)
    ]

    def score(j, best, masked):
        start = pl.multiple_of(j * KEY_BLOCK, 128)
        result = []
        for group in range(2):
            part = lax.dot_general(
                rows[group],
                key[pl.ds(start, KEY_BLOCK), :],
                (((1,), (1,)), ((), ())),
                preferred_element_type=jnp.float32,
            )
            top = best[group]
            for t in range(LANES):
                piece = part[:, t * 128 : (t + 1) * 128]
                if masked:
                    piece = jnp.where(key_pos <= query_pos - (start + t * 128), piece, -1e30)
                scores[group, j, :, t * 128 : (t + 1) * 128] = piece
                top = jnp.maximum(top, piece)
            result.append(top)
        return tuple(result)

    low = jnp.full((GROUP, 128), -1e30, jnp.float32)

    best = lax.fori_loop(0, blocks, lambda j, b: score(j, b, True), (low, low))
    tops = [jnp.broadcast_to(jnp.max(b, axis=-1, keepdims=True), (GROUP, 128)) for b in best]

    def mix(j, totals):
        start = pl.multiple_of(j * KEY_BLOCK, 128)
        result = []
        for group in range(2):
            weights = jnp.concatenate(
                [
                    jnp.exp2((scores[group, j, :, t * 128 : (t + 1) * 128] - tops[group]) * gain).astype(
                        jnp.bfloat16
                    )
                    for t in range(LANES)
                ],
                1,
            )
            result.append(
                totals[group]
                + jnp.dot(
                    weights, wide[pl.ds(start, KEY_BLOCK), :], preferred_element_type=jnp.float32
                )
            )
        return tuple(result)

    none = jnp.zeros((GROUP, 2 * HEAD), jnp.float32)
    totals = lax.fori_loop(0, blocks, mix, (none, none))
    for group in range(2):
        normed = (totals[group][:, :HEAD] / totals[group][:, HEAD:]).astype(jnp.bfloat16)
        for h in range(2):
            column = (2 * group + h) * HEAD
            o_ref[:, column : column + HEAD] = normed[h * TOKENS : (h + 1) * TOKENS]


VMEM = pl.BlockSpec(memory_space=pltpu.VMEM)
SMEM = pl.BlockSpec(memory_space=pltpu.SMEM)
ANY = pl.BlockSpec(memory_space=pl.ANY)


HBM = pl.BlockSpec(memory_space=pltpu.HBM)


def attention(place, queries, held, swapped):
    return pl.pallas_call(
        attention_kernel,
        out_shape=jax.ShapeDtypeStruct((TOKENS, WIDTH), jnp.bfloat16),
        in_specs=[SMEM, HBM, VMEM, VMEM],
        out_specs=VMEM,
        scratch_shapes=[
            pltpu.VMEM((KEYS, HEAD), jnp.bfloat16),
            pltpu.VMEM((KEYS, 2 * HEAD), jnp.bfloat16),
            pltpu.VMEM((2, KEYS // KEY_BLOCK, GROUP, KEY_BLOCK), jnp.float32),
            pltpu.VMEM((TOKENS, WIDTH), jnp.bfloat16),
            pltpu.SemaphoreType.DMA,
        ],
        compiler_params=pltpu.CompilerParams(vmem_limit_bytes=30 << 20),
        cost_estimate=pl.CostEstimate(
            flops=8 * GROUP * KEYS * HEAD, bytes_accessed=3 << 20, transcendentals=2 * GROUP * KEYS
        ),
        name="attend",
    )(place, queries, held, swapped)


def project_kernel(
    place_ref, mine_ref, theirs_ref, own_hbm, other_hbm, sign_ref, turn_ref, spread_ref, *refs
):
    o_refs, (own, other, sems) = refs[: 2 * CHIPS], refs[2 * CHIPS :]
    core, chip = place_ref[1], place_ref[2]

    def column(step):
        distance = 4 - (step + 1) // 2
        offset = jnp.where(lax.rem(step, 2) == 0, -distance, distance)
        return lax.rem(chip + offset + CHIPS, CHIPS) * CHUNK + core * SHARE

    def fetches(step):
        start = pl.multiple_of(column(step), SHARE)
        return [
            pltpu.make_async_copy(
                source.at[:, pl.ds(start, SHARE)], target.at[step], sems.at[n, step]
            )
            for n, (source, target) in enumerate(((own_hbm, own), (other_hbm, other)))
        ]

    @pl.loop(0, CHIPS)
    def _(step):
        for fetch in fetches(step):
            fetch.start()

    @pl.loop(0, CHIPS)
    def _(step):
        for fetch in fetches(step):
            fetch.wait()
        start = pl.multiple_of(column(step), SHARE)
        totals = []
        for half in range(2):
            columns = slice(half * COLS, (half + 1) * COLS)
            signs = (2 * sign_ref[:, pl.ds(start + half * COLS, COLS)] - 1).astype(jnp.float32)
            totals.append(
                clipped_partial(
                    ((mine_ref[...], own[step, :, columns]), (theirs_ref[...], other[step, :, columns])),
                    signs,
                    turn_ref,
                    spread_ref,
                )
            )
        for n in range(CHIPS):

            @pl.when(step == n)
            def _(n=n):
                for half in range(2):
                    o_ref = o_refs[2 * n + half]
                    for b in range(SUB):
                        piece = totals[half][:, b * BLOCK : (b + 1) * BLOCK]
                        o_ref[b * TOKENS : (b + 1) * TOKENS, :] = piece.astype(o_ref.dtype)


def project(place, mine, theirs, own, other, signs, turn, spread):
    half = jax.ShapeDtypeStruct((ROWS, BLOCK), jnp.bfloat16)
    full = jax.ShapeDtypeStruct((ROWS, BLOCK), jnp.float32)
    return pl.pallas_call(
        project_kernel,
        out_shape=(half,) * (2 * CHIPS - 2) + (full,) * 2,
        in_specs=[SMEM, VMEM, VMEM, HBM, HBM, VMEM, VMEM, VMEM],
        out_specs=(VMEM,) * (2 * CHIPS),
        scratch_shapes=[
            pltpu.VMEM((CHIPS, WIDTH, SHARE), jnp.bfloat16),
            pltpu.VMEM((CHIPS, WIDTH, SHARE), jnp.bfloat16),
            pltpu.SemaphoreType.DMA((2, CHIPS)),
        ],
        compiler_params=pltpu.CompilerParams(vmem_limit_bytes=50 << 20),
        cost_estimate=pl.CostEstimate(
            flops=2 * TOKENS * 1280 * D // 2, bytes_accessed=10 << 20, transcendentals=0
        ),
        name="project",
    )(place, mine, theirs, own, other, signs, turn, spread)


def pack_kernel(own0, own1, up0, up1, down0, down1, o0_ref, o1_ref, square):
    for own, up, down, out in ((own0, up0, down0, o0_ref), (own1, up1, down1, o1_ref)):
        lane = lax.broadcasted_iota(jnp.int32, (TOKENS, BLOCK), 1)
        columns = jnp.zeros((TOKENS, BLOCK), jnp.float32)
        for b in range(SUB):
            rows = slice(b * TOKENS, (b + 1) * TOKENS)
            came = up[rows, :].astype(jnp.float32) + down[rows, :].astype(jnp.float32)
            summed = (own[rows, :] + came) * (1.0 / math.sqrt(BLOCK))
            scale = jnp.max(jnp.abs(summed), axis=-1, keepdims=True) + 1e-06
            out[rows, :] = (summed / scale).astype(jnp.bfloat16)
            columns = jnp.where(lane == b, scale, columns)
        square[...] = jnp.zeros((2 * BLOCK, BLOCK), jnp.float32)
        square[:TOKENS, :] = columns
        turned = jnp.concatenate(
            [square[:BLOCK, :].T[:SUB, :], square[BLOCK:, :].T[:SUB, :]], 0
        )
        upper = turned.astype(jnp.bfloat16).astype(jnp.float32)
        tail = jnp.concatenate([upper, turned - upper, jnp.zeros((8, BLOCK), jnp.float32)], 0)
        out[ROWS:, :] = tail.astype(jnp.bfloat16)


def pack(own, up, down):
    shape = jax.ShapeDtypeStruct((MSG, BLOCK), jnp.bfloat16)
    return pl.pallas_call(
        pack_kernel,
        out_shape=(shape, shape),
        in_specs=[VMEM] * 6,
        out_specs=(VMEM, VMEM),
        scratch_shapes=[pltpu.VMEM((2 * BLOCK, BLOCK), jnp.float32)],
        compiler_params=pltpu.CompilerParams(vmem_limit_bytes=8 << 20),
        cost_estimate=pl.CostEstimate(flops=1 << 20, bytes_accessed=1 << 20, transcendentals=0),
        name="pack",
    )(*own, *up, *down)


def assemble_kernel(places, fresh, last, index_ref, *refs):
    count = 1 + max(place[0] for place in places)
    arrays, refs = refs[:count], refs[count:]
    joined = []
    if fresh:
        out_ref, table, joined_ref, tails, sems, tail_sems, join_sems = refs
        for n in range(count):
            joined.append(
                pltpu.make_async_copy(
                    arrays[n], joined_ref.at[pl.ds(n * MSG, MSG), :], join_sems.at[n]
                )
            )
            joined[-1].start()
    else:
        _, old_table, out_ref, table, tails, sems, tail_sems = refs[:7]
        if last:
            _, _, out_ref, scale_ref, table, tails, sems, tail_sems = refs
        table[...] = old_table[...]
    core, chip = index_ref[0], index_ref[1]

    def spot(swap, offset):
        side = (1 - core) if swap else core
        return side, lax.rem(chip + offset + CHIPS, CHIPS)

    copies, tail_copies = [], []
    for n, (array, row, swap, offset, half) in enumerate(places):
        tail_copies.append(
            pltpu.make_async_copy(
                arrays[array].at[pl.ds(row + ROWS, 16), :], tails.at[n], tail_sems.at[n]
            )
        )
        tail_copies[-1].start()
    for n, (array, row, swap, offset, half) in enumerate(places):
        side, place = spot(swap, offset)
        for b in range(SUB):
            column = pl.multiple_of(place * CHUNK + side * SHARE + half * COLS + b * BLOCK, BLOCK)
            copies.append(
                pltpu.make_async_copy(
                    arrays[array].at[pl.ds(row + b * TOKENS, TOKENS), :],
                    out_ref.at[:, pl.ds(column, BLOCK)],
                    sems.at[n * SUB + b],
                )
            )
            copies[-1].start()
    for n, (array, row, swap, offset, half) in enumerate(places):
        tail_copies[n].wait()
        side, place = spot(swap, offset)
        tail = tails[n].astype(jnp.float32)
        tail = tail[: 2 * SUB] + tail[2 * SUB : 4 * SUB]
        for t in range(2):
            table[place, side, half * SUB : (half + 1) * SUB, t * BLOCK : (t + 1) * BLOCK] = tail[
                t * SUB : (t + 1) * SUB
            ]
    if last:
        for place in range(CHIPS):
            for side in range(2):
                row = (2 * place + side) * 2 * SUB
                scale_ref[row : row + 2 * SUB, :] = table[place, side][:, :TOKENS]
    for copy in joined + copies:
        copy.wait()


def assemble(index, arrays, places, before, last):
    table_shape = (CHIPS, 2, 2 * SUB, 2 * BLOCK)
    out_shape = [jax.ShapeDtypeStruct((TOKENS, D), jnp.bfloat16)]
    out_shape.append(
        jax.ShapeDtypeStruct((D // BLOCK, TOKENS) if last else table_shape, jnp.float32)
    )
    scratch = [pltpu.VMEM(table_shape, jnp.float32)] if last else []
    fresh = before is None
    out_specs, more = [ANY, VMEM], []
    if fresh:
        out_shape.append(jax.ShapeDtypeStruct((len(arrays) * MSG, BLOCK), jnp.bfloat16))
        out_specs.append(ANY)
        more = [pltpu.SemaphoreType.DMA((len(arrays),))]
    payload = pl.pallas_call(
        functools.partial(assemble_kernel, places, fresh, last),
        out_shape=tuple(out_shape),
        in_specs=[SMEM] + [ANY] * len(arrays) + ([] if fresh else [ANY, VMEM]),
        out_specs=tuple(out_specs),
        scratch_shapes=scratch
        + [
            pltpu.VMEM((len(places), 16, BLOCK), jnp.bfloat16),
            pltpu.SemaphoreType.DMA((len(places) * SUB,)),
            pltpu.SemaphoreType.DMA((len(places),)),
            *more,
        ],
        input_output_aliases={} if fresh else {len(arrays) + 1: 0},
        compiler_params=pltpu.CompilerParams(vmem_limit_bytes=4 << 20),
        cost_estimate=pl.CostEstimate(flops=1 << 20, bytes_accessed=4 << 20, transcendentals=0),
        name="assemble",
    )(index, *arrays, *([] if fresh else before))
    return (payload[2], *payload[:2]) if fresh else payload


def add(arrived, own):
    return (arrived.astype(jnp.float32) + own.astype(jnp.float32)).astype(jnp.bfloat16)


def send(x, pairs):
    return lax.ppermute(x, "tp", pairs)


EARLY = 12


def layer(queries, keys, values, out_weight, signs):
    ctx, tp = lax.axis_index("ctx"), lax.axis_index("tp")
    core, chip = tp & 1, tp >> 1

    place = jnp.stack([ctx * TOKENS, core, chip, ctx >> 2, ctx & 3]).astype(jnp.int32)

    other_weight = send(out_weight, PAIR)

    def spread_out(x, pairs):
        up, down = (lax.ppermute(x, ("ctx", "tp"), way) for way in pairs)
        count = x.shape[0] // 2
        if count < TOKENS:
            far = (lax.ppermute(up, ("ctx", "tp"), pairs[0]),)
        else:
            far = (
                lax.ppermute(up[:count], ("ctx", "tp"), pairs[0]),
                lax.ppermute(down[count:], ("ctx", "tp"), pairs[1]),
            )
        return jnp.concatenate([x, up, down, *far], 0)

    key_part = lax.dynamic_slice_in_dim(keys, chip * HEAD, HEAD, 1)
    value_part = lax.dynamic_slice_in_dim(values, chip * HEAD, HEAD, 1)
    held = spread_out(jnp.where(core == 0, key_part, value_part), FIRST)
    held = spread_out(held, SECOND)
    swapped = send(held, PAIR)

    index = jnp.stack([core, chip]).astype(jnp.int32)
    turn = jnp.asarray(turn_matrix(), jnp.bfloat16)
    spread = jnp.asarray(spread_matrix(), jnp.bfloat16)
    attended = attention(place, queries, held, swapped)
    parts = project(
        place,
        attended,
        send(attended, PAIR),
        out_weight,
        other_weight,
        signs[None, :],
        turn,
        spread,
    )

    def plus(arrived, up, down):
        arrived = lax.optimization_barrier(arrived)
        return add(arrived[0], up), add(arrived[1], down)

    def both_ways(up, down):
        up = send(up, UP)
        down = send(down, DOWN)
        return up, down

    a = both_ways(parts[0], parts[1])
    b = both_ways(parts[3], parts[4])
    a = both_ways(*plus(a, parts[2], parts[5]))
    for near in (6, 10):
        b = both_ways(*plus(b, parts[near + 1], parts[near + 2]))
        a = both_ways(*plus(a, parts[near], parts[near + 3]))
    packed = pack(parts[14:], (a[0], b[0]), (b[1], a[1]))

    pieces, spots = list(packed), [(0, 0), (0, 1)]
    chains = [(packed[0], packed[1]), (packed[1], packed[0])]
    for step in range(7):
        h, hop = step % 2, step // 2 + 1
        chains[h] = both_ways(*lax.optimization_barrier(chains[h]))
        pieces += chains[h]
        spots += [(-hop, h), (hop, 1 - h)]

    def rows(swap, a, b, joined):
        return tuple(
            (0 if joined else n - a, (n - a) * MSG if joined else 0, swap, *spots[n])
            for n in range(a, b)
        )

    first = assemble(index, pieces[:EARLY], rows(False, 0, EARLY, False), None, False)
    early, *first = first
    early = send(early, PAIR)
    rest = jnp.concatenate(pieces[EARLY:], 0)
    late = send(rest, PAIR)
    second = assemble(index, [early], rows(True, 0, EARLY, True), first, False)
    count = len(pieces) - EARLY
    tail = rows(False, EARLY, EARLY + count, True) + tuple(
        (1, *where[1:]) for where in rows(True, EARLY, EARLY + count, True)
    )
    payload, scales = assemble(index, [rest, late], tail, second, True)
    return payload, scales.T


def solution(mesh):
    return jax.shard_map(
        layer,
        mesh=mesh,
        in_specs=(P("ctx", "tp"), P("ctx", None), P("ctx", None), P("tp", None), P()),
        out_specs=(P("ctx", None), P("ctx", None)),
        check_vma=False,
    )
```

```python
import functools
import math

import jax
import jax.numpy as jnp
import numpy as np
from jax import lax
from jax.experimental import pallas as pl
from jax.experimental.pallas import tpu as pltpu
from jax.sharding import PartitionSpec as P


D = 8192
HEAD = 128
BLOCK = 128
CHIPS = 8
TOKENS = 224
HEADS = 4
WIDTH = HEADS * HEAD
KEYS = 3584
KEY_BLOCK = 896
CHUNK = D // CHIPS
SHARE = CHUNK // 2
COLS = SHARE // 2
SUB = COLS // BLOCK
ROWS = SUB * TOKENS
MSG = ROWS + 16

WAY_A = [(t, (t + 2 if t // 2 % 2 == 0 else t - 2) % 16) for t in range(16)]
WAY_B = [(t, (t - 2 if t // 2 % 2 == 0 else t + 2) % 16) for t in range(16)]
PAIR = [(t, t ^ 1) for t in range(16)]

SIDE = 4


def torus_pairs(axis_of_core, step):
    pairs = []
    for c in range(SIDE * SIDE):
        for t in range(16):
            y, x = divmod(c, SIDE)
            if axis_of_core[t % 2] == "x":
                x = (x + step) % SIDE
            else:
                y = (y + step) % SIDE
            pairs.append((c * 16 + t, (y * SIDE + x) * 16 + t))
    return pairs


FIRST = torus_pairs("xy", 1), torus_pairs("xy", -1)
SECOND = torus_pairs("yx", 1), torus_pairs("yx", -1)


def turn_matrix():
    common = np.arange(BLOCK)[:, None] & np.arange(BLOCK)[None, :]
    parity = np.zeros((BLOCK, BLOCK), np.int64)
    for bit in range(BLOCK.bit_length() - 1):
        parity += (common >> bit) & 1
    return np.kron(np.eye(2), 1 - 2 * (parity % 2)).astype(np.float32)


def spread_matrix():
    row, column = np.arange(BLOCK)[:, None], np.arange(COLS)[None, :]
    return ((row % SUB == column // BLOCK) & (row < 2 * SUB)).astype(np.float32)


def clipped_partial(pairs, signs, turn_ref, spread_ref):
    flat = jnp.concatenate(
        [
            (jnp.dot(rows, weight, preferred_element_type=jnp.float32) * signs).astype(jnp.bfloat16)
            for rows, weight in pairs
        ],
        0,
    )
    squares = lax.dot_general(
        flat * flat, spread_ref[...], (((1,), (1,)), ((), ())), preferred_element_type=jnp.float32
    )
    limit = 2.0 * jnp.sqrt(squares + BLOCK * 1e-06)
    upper = limit.astype(jnp.bfloat16).astype(jnp.float32)
    lane = lax.broadcasted_iota(jnp.int32, limit.shape, 1)
    limit = jnp.where(lane < SUB, upper, limit - upper).astype(jnp.bfloat16)
    limit = jnp.dot(limit, spread_ref[...], preferred_element_type=jnp.float32)
    turned = jnp.dot(flat, turn_ref[...], preferred_element_type=jnp.float32)
    clipped = jnp.minimum(jnp.maximum(turned, -limit), limit)
    return clipped[:TOKENS] + clipped[TOKENS:]


GROUP = HEADS // 2 * TOKENS
LANES = KEY_BLOCK // 128


def attention_kernel(place_ref, query_hbm, held_ref, swapped_ref, o_ref, key, wide, scores, query_ref, sem):
    first, core, y, x = place_ref[0], place_ref[1], place_ref[3], place_ref[4]
    fetch = pltpu.make_async_copy(query_hbm, query_ref, sem)
    fetch.start()
    blocks = (first + TOKENS - 1) // KEY_BLOCK + 1
    gain = math.log2(math.e) / math.sqrt(HEAD)

    def sort(keys_ref, values_ref):
        @pl.loop(0, SIDE * SIDE)
        def _(n):
            far, near = (
                jnp.where(i == 1, SIDE - 1, jnp.maximum(i - 1, 0)) for i in (n // SIDE, lax.rem(n, SIDE))
            )
            block = pl.multiple_of(n * TOKENS, 32)
            row, column = lax.rem(y + far, SIDE), lax.rem(x + near, SIDE)
            start = pl.multiple_of((row * SIDE + column) * TOKENS, 32)
            key[pl.ds(start, TOKENS), :] = keys_ref[pl.ds(block, TOKENS), :]
            row, column = lax.rem(y + near, SIDE), lax.rem(x + far, SIDE)
            start = pl.multiple_of((row * SIDE + column) * TOKENS, 32)
            wide[pl.ds(start, TOKENS), :HEAD] = values_ref[pl.ds(block, TOKENS), :]

    @pl.when(core == 0)
    def _():
        sort(held_ref, swapped_ref)

    @pl.when(core != 0)
    def _():
        sort(swapped_ref, held_ref)

    wide[:, HEAD:] = jnp.ones((KEYS, HEAD), jnp.bfloat16)
    fetch.wait()
    query_pos = first + lax.rem(
        lax.broadcasted_iota(jnp.int32, (GROUP, 128), 0), TOKENS
    )
    key_pos = lax.broadcasted_iota(jnp.int32, (GROUP, 128), 1)
    rows = [
        jnp.concatenate([query_ref[:, h * HEAD : (h + 1) * HEAD] for h in (2 * g, 2 * g + 1)], 0)
        for g in range(2)
    ]

    def score(j, best, masked):
        start = pl.multiple_of(j * KEY_BLOCK, 128)
        result = []
        for group in range(2):
            part = lax.dot_general(
                rows[group],
                key[pl.ds(start, KEY_BLOCK), :],
                (((1,), (1,)), ((), ())),
                preferred_element_type=jnp.float32,
            )
            top = best[group]
            for t in range(LANES):
                piece = part[:, t * 128 : (t + 1) * 128]
                if masked:
                    piece = jnp.where(key_pos <= query_pos - (start + t * 128), piece, -1e30)
                scores[group, j, :, t * 128 : (t + 1) * 128] = piece
                top = jnp.maximum(top, piece)
            result.append(top)
        return tuple(result)

    low = jnp.full((GROUP, 128), -1e30, jnp.float32)

    best = lax.fori_loop(0, blocks, lambda j, b: score(j, b, True), (low, low))
    tops = [jnp.broadcast_to(jnp.max(b, axis=-1, keepdims=True), (GROUP, 128)) for b in best]

    def mix(j, totals):
        start = pl.multiple_of(j * KEY_BLOCK, 128)
        result = []
        for group in range(2):
            weights = jnp.concatenate(
                [
                    jnp.exp2((scores[group, j, :, t * 128 : (t + 1) * 128] - tops[group]) * gain).astype(
                        jnp.bfloat16
                    )
                    for t in range(LANES)
                ],
                1,
            )
            result.append(
                totals[group]
                + jnp.dot(
                    weights, wide[pl.ds(start, KEY_BLOCK), :], preferred_element_type=jnp.float32
                )
            )
        return tuple(result)

    none = jnp.zeros((GROUP, 2 * HEAD), jnp.float32)
    totals = lax.fori_loop(0, blocks, mix, (none, none))
    for group in range(2):
        normed = (totals[group][:, :HEAD] / totals[group][:, HEAD:]).astype(jnp.bfloat16)
        for h in range(2):
            column = (2 * group + h) * HEAD
            o_ref[:, column : column + HEAD] = normed[h * TOKENS : (h + 1) * TOKENS]


VMEM = pl.BlockSpec(memory_space=pltpu.VMEM)
SMEM = pl.BlockSpec(memory_space=pltpu.SMEM)
ANY = pl.BlockSpec(memory_space=pl.ANY)


HBM = pl.BlockSpec(memory_space=pltpu.HBM)


def attention(place, queries, held, swapped):
    return pl.pallas_call(
        attention_kernel,
        out_shape=jax.ShapeDtypeStruct((TOKENS, WIDTH), jnp.bfloat16),
        in_specs=[SMEM, HBM, VMEM, VMEM],
        out_specs=VMEM,
        scratch_shapes=[
            pltpu.VMEM((KEYS, HEAD), jnp.bfloat16),
            pltpu.VMEM((KEYS, 2 * HEAD), jnp.bfloat16),
            pltpu.VMEM((2, KEYS // KEY_BLOCK, GROUP, KEY_BLOCK), jnp.float32),
            pltpu.VMEM((TOKENS, WIDTH), jnp.bfloat16),
            pltpu.SemaphoreType.DMA,
        ],
        compiler_params=pltpu.CompilerParams(vmem_limit_bytes=30 << 20),
        cost_estimate=pl.CostEstimate(
            flops=8 * GROUP * KEYS * HEAD, bytes_accessed=3 << 20, transcendentals=2 * GROUP * KEYS
        ),
        name="attend",
    )(place, queries, held, swapped)


def project_kernel(
    place_ref, mine_ref, theirs_ref, own_hbm, other_hbm, sign_ref, turn_ref, spread_ref, *refs
):
    o_refs, (own, other, sems) = refs[: CHIPS + 1], refs[CHIPS + 1 :]
    core, chip, way = place_ref[1], place_ref[2], place_ref[5]

    def column(step):
        distance = 4 - (step + 1) // 2
        offset = way * jnp.where(lax.rem(step, 2) == 0, -distance, distance)
        return lax.rem(chip + offset + CHIPS, CHIPS) * CHUNK + core * SHARE

    def fetches(step):
        start = pl.multiple_of(column(step), SHARE)
        return [
            pltpu.make_async_copy(
                source.at[:, pl.ds(start, SHARE)], target.at[step], sems.at[n, step]
            )
            for n, (source, target) in enumerate(((own_hbm, own), (other_hbm, other)))
        ]

    @pl.loop(0, CHIPS)
    def _(step):
        for fetch in fetches(step):
            fetch.start()

    @pl.loop(0, CHIPS)
    def _(step):
        for fetch in fetches(step):
            fetch.wait()
        start = pl.multiple_of(column(step), SHARE)
        totals = []
        for half in range(2):
            columns = slice(half * COLS, (half + 1) * COLS)
            signs = (2 * sign_ref[:, pl.ds(start + half * COLS, COLS)] - 1).astype(jnp.float32)
            totals.append(
                clipped_partial(
                    ((mine_ref[...], own[step, :, columns]), (theirs_ref[...], other[step, :, columns])),
                    signs,
                    turn_ref,
                    spread_ref,
                )
            )
        for n in range(CHIPS):

            @pl.when(step == n)
            def _(n=n):
                for half in range(2):
                    o_ref, row = (o_refs[half], 0) if n == 0 else (o_refs[n + 1], half * ROWS)
                    for b in range(SUB):
                        piece = totals[half][:, b * BLOCK : (b + 1) * BLOCK]
                        o_ref[row + b * TOKENS : row + (b + 1) * TOKENS, :] = piece.astype(o_ref.dtype)


def project(place, mine, theirs, own, other, signs, turn, spread):
    half = jax.ShapeDtypeStruct((ROWS, BLOCK), jnp.bfloat16)
    both = jax.ShapeDtypeStruct((2 * ROWS, BLOCK), jnp.bfloat16)
    full = jax.ShapeDtypeStruct((2 * ROWS, BLOCK), jnp.float32)
    return pl.pallas_call(
        project_kernel,
        out_shape=(half,) * 2 + (both,) * (CHIPS - 2) + (full,),
        in_specs=[SMEM, VMEM, VMEM, HBM, HBM, VMEM, VMEM, VMEM],
        out_specs=(VMEM,) * (CHIPS + 1),
        scratch_shapes=[
            pltpu.VMEM((CHIPS, WIDTH, SHARE), jnp.bfloat16),
            pltpu.VMEM((CHIPS, WIDTH, SHARE), jnp.bfloat16),
            pltpu.SemaphoreType.DMA((2, CHIPS)),
        ],
        compiler_params=pltpu.CompilerParams(vmem_limit_bytes=50 << 20),
        cost_estimate=pl.CostEstimate(
            flops=2 * TOKENS * 1280 * D // 2, bytes_accessed=10 << 20, transcendentals=0
        ),
        name="project",
    )(place, mine, theirs, own, other, signs, turn, spread)


def pack_kernel(own, one, two, out, square):
    for half in range(2):
        lane = lax.broadcasted_iota(jnp.int32, (TOKENS, BLOCK), 1)
        columns = jnp.zeros((TOKENS, BLOCK), jnp.float32)
        for b in range(SUB):
            rows = slice(half * ROWS + b * TOKENS, half * ROWS + (b + 1) * TOKENS)
            came = one[rows, :].astype(jnp.float32) + two[rows, :].astype(jnp.float32)
            summed = (own[rows, :] + came) * (1.0 / math.sqrt(BLOCK))
            scale = jnp.max(jnp.abs(summed), axis=-1, keepdims=True) + 1e-06
            to = half * MSG + b * TOKENS
            out[to : to + TOKENS, :] = (summed / scale).astype(jnp.bfloat16)
            columns = jnp.where(lane == b, scale, columns)
        square[...] = jnp.zeros((2 * BLOCK, BLOCK), jnp.float32)
        square[:TOKENS, :] = columns
        turned = jnp.concatenate(
            [square[:BLOCK, :].T[:SUB, :], square[BLOCK:, :].T[:SUB, :]], 0
        )
        upper = turned.astype(jnp.bfloat16).astype(jnp.float32)
        tail = jnp.concatenate([upper, turned - upper, jnp.zeros((8, BLOCK), jnp.float32)], 0)
        out[half * MSG + ROWS : (half + 1) * MSG, :] = tail.astype(jnp.bfloat16)


def pack(own, one, two):
    return pl.pallas_call(
        pack_kernel,
        out_shape=jax.ShapeDtypeStruct((2 * MSG, BLOCK), jnp.bfloat16),
        in_specs=[VMEM] * 3,
        out_specs=VMEM,
        scratch_shapes=[pltpu.VMEM((2 * BLOCK, BLOCK), jnp.float32)],
        compiler_params=pltpu.CompilerParams(vmem_limit_bytes=8 << 20),
        cost_estimate=pl.CostEstimate(flops=1 << 20, bytes_accessed=1 << 20, transcendentals=0),
        name="pack",
    )(own, one, two)


def assemble_kernel(places, fresh, last, index_ref, *refs):
    count = 1 + max(place[0] for place in places)
    arrays, refs = refs[:count], refs[count:]
    if fresh:
        out_ref, table, tails, sems, tail_sems = refs
    else:
        _, old_table, out_ref, table, tails, sems, tail_sems = refs[:7]
        if last:
            _, _, out_ref, scale_ref, table, tails, sems, tail_sems = refs
        table[...] = old_table[...]
    core, chip, way = index_ref[1], index_ref[2], index_ref[5]

    def spot(swap, offset):
        side = (1 - core) if swap else core
        return side, lax.rem(chip + way * offset + CHIPS, CHIPS)

    copies, tail_copies = [], []
    for n, (array, row, swap, offset, half) in enumerate(places):
        tail_copies.append(
            pltpu.make_async_copy(
                arrays[array].at[pl.ds(row + ROWS, 16), :], tails.at[n], tail_sems.at[n]
            )
        )
        tail_copies[-1].start()
    for n, (array, row, swap, offset, half) in enumerate(places):
        side, place = spot(swap, offset)
        for b in range(SUB):
            column = pl.multiple_of(place * CHUNK + side * SHARE + half * COLS + b * BLOCK, BLOCK)
            copies.append(
                pltpu.make_async_copy(
                    arrays[array].at[pl.ds(row + b * TOKENS, TOKENS), :],
                    out_ref.at[:, pl.ds(column, BLOCK)],
                    sems.at[n * SUB + b],
                )
            )
            copies[-1].start()
    for n, (array, row, swap, offset, half) in enumerate(places):
        tail_copies[n].wait()
        side, place = spot(swap, offset)
        tail = tails[n].astype(jnp.float32)
        tail = tail[: 2 * SUB] + tail[2 * SUB : 4 * SUB]
        for t in range(2):
            table[place, side, half * SUB : (half + 1) * SUB, t * BLOCK : (t + 1) * BLOCK] = tail[
                t * SUB : (t + 1) * SUB
            ]
    if last:
        for place in range(CHIPS):
            for side in range(2):
                row = (2 * place + side) * 2 * SUB
                scale_ref[row : row + 2 * SUB, :] = table[place, side][:, :TOKENS]
    for copy in copies:
        copy.wait()


def assemble(index, arrays, places, before, last):
    table_shape = (CHIPS, 2, 2 * SUB, 2 * BLOCK)
    out_shape = [jax.ShapeDtypeStruct((TOKENS, D), jnp.bfloat16)]
    out_shape.append(
        jax.ShapeDtypeStruct((D // BLOCK, TOKENS) if last else table_shape, jnp.float32)
    )
    scratch = [pltpu.VMEM(table_shape, jnp.float32)] if last else []
    fresh = before is None
    return pl.pallas_call(
        functools.partial(assemble_kernel, places, fresh, last),
        out_shape=tuple(out_shape),
        in_specs=[SMEM] + [ANY] * len(arrays) + ([] if fresh else [ANY, VMEM]),
        out_specs=(ANY, VMEM),
        scratch_shapes=scratch
        + [
            pltpu.VMEM((len(places), 16, BLOCK), jnp.bfloat16),
            pltpu.SemaphoreType.DMA((len(places) * SUB,)),
            pltpu.SemaphoreType.DMA((len(places),)),
        ],
        input_output_aliases={} if fresh else {len(arrays) + 1: 0},
        compiler_params=pltpu.CompilerParams(vmem_limit_bytes=4 << 20),
        cost_estimate=pl.CostEstimate(flops=1 << 20, bytes_accessed=4 << 20, transcendentals=0),
        name="assemble",
    )(index, *arrays, *([] if fresh else before))


def add(arrived, own):
    return (arrived.astype(jnp.float32) + own.astype(jnp.float32)).astype(jnp.bfloat16)


def send(x, pairs):
    return lax.ppermute(x, "tp", pairs)


def layer(queries, keys, values, out_weight, signs):
    ctx, tp = lax.axis_index("ctx"), lax.axis_index("tp")
    core, chip = tp & 1, tp >> 1

    place = jnp.stack(
        [ctx * TOKENS, core, chip, ctx >> 2, ctx & 3, 1 - 2 * (chip & 1)]
    ).astype(jnp.int32)

    other_weight = send(out_weight, PAIR)

    def spread_out(x, pairs):
        up, down = (lax.ppermute(x, ("ctx", "tp"), way) for way in pairs)
        count = x.shape[0] // 2
        if count < TOKENS:
            far = (lax.ppermute(up, ("ctx", "tp"), pairs[0]),)
        else:
            far = (
                lax.ppermute(up[:count], ("ctx", "tp"), pairs[0]),
                lax.ppermute(down[count:], ("ctx", "tp"), pairs[1]),
            )
        return jnp.concatenate([x, up, down, *far], 0)

    key_part = lax.dynamic_slice_in_dim(keys, chip * HEAD, HEAD, 1)
    value_part = lax.dynamic_slice_in_dim(values, chip * HEAD, HEAD, 1)
    held = spread_out(jnp.where(core == 0, key_part, value_part), FIRST)
    held = spread_out(held, SECOND)
    swapped = send(held, PAIR)

    turn = jnp.asarray(turn_matrix(), jnp.bfloat16)
    spread = jnp.asarray(spread_matrix(), jnp.bfloat16)
    attended = attention(place, queries, held, swapped)
    parts = project(
        place,
        attended,
        send(attended, PAIR),
        out_weight,
        other_weight,
        signs[None, :],
        turn,
        spread,
    )

    def exchange(for_a, for_b):
        came_b = send(for_a, WAY_A)
        came_a = send(for_b, WAY_B)
        return came_a, came_b

    came_a, came_b = exchange(parts[0], parts[1])
    for_a, for_b = parts[2], parts[3]
    for_a = lax.dynamic_update_slice(for_a, add(came_a, for_a[ROWS:]), (ROWS, 0))
    for_b = lax.dynamic_update_slice(for_b, add(came_b, for_b[:ROWS]), (0, 0))
    came_a, came_b = exchange(for_a, for_b)
    came_a, came_b = exchange(add(came_a, parts[4]), add(came_b, parts[5]))
    came_a, came_b = exchange(add(came_a, parts[6]), add(came_b, parts[7]))
    packed = pack(parts[8], came_a, came_b)

    stages = [[(packed, 0, None)]]
    came_a = came_b = packed
    for hop in range(1, 5):
        if hop < 4:
            came_a, came_b = exchange(came_a, came_b)
            stages.append([(came_a, -hop, None), (came_b, hop, None)])
        else:
            came_a, came_b = exchange(came_a[:MSG], came_b[MSG:])
            stages.append([(came_a, hop, 1), (came_b, hop, 0)])
    swapped_stages = []
    for stage in stages:
        swapped_stages.append([(send(array, PAIR), *rest) for array, *rest in stage])

    def gather(hops, before, last=False):
        arrays, places = [], []
        for swap, source in ((False, stages), (True, swapped_stages)):
            for hop in hops:
                for array, offset, half in source[hop]:
                    for h in (0, 1) if half is None else (half,):
                        row = h * MSG if half is None else 0
                        places.append((len(arrays), row, swap, offset, h))
                    arrays.append(array)
        return assemble(place, arrays, tuple(places), before, last)

    result = gather((0, 1), None)
    result = gather((2,), result)
    result = gather((3,), result)
    payload, scales = gather((4,), result, True)
    return payload, scales.T


def solution(mesh):
    return jax.shard_map(
        layer,
        mesh=mesh,
        in_specs=(P("ctx", "tp"), P("ctx", None), P("ctx", None), P("tp", None), P()),
        out_specs=(P("ctx", None), P("ctx", None)),
        check_vma=False,
    )
```

```python
import functools
import math

import jax
import jax.numpy as jnp
import numpy as np
from jax import lax
from jax.experimental import pallas as pl
from jax.experimental.pallas import tpu as pltpu
from jax.sharding import PartitionSpec as P


D = 8192
HEAD = 128
BLOCK = 128
CHIPS = 8
TOKENS = 224
HEADS = 4
WIDTH = HEADS * HEAD
KEYS = 3584
KEY_BLOCK = 896
CHUNK = D // CHIPS
SHARE = CHUNK // 2
COLS = SHARE // 2
SUB = COLS // BLOCK
ROWS = SUB * TOKENS
MSG = ROWS + 16

WAY_A = [(t, (t + 2 if t // 2 % 2 == 0 else t - 2) % 16) for t in range(16)]
WAY_B = [(t, (t - 2 if t // 2 % 2 == 0 else t + 2) % 16) for t in range(16)]
PAIR = [(t, t ^ 1) for t in range(16)]

SIDE = 4


def torus_pairs(axis_of_core, step):
    pairs = []
    for c in range(SIDE * SIDE):
        for t in range(16):
            y, x = divmod(c, SIDE)
            if axis_of_core[t % 2] == "x":
                x = (x + step) % SIDE
            else:
                y = (y + step) % SIDE
            pairs.append((c * 16 + t, (y * SIDE + x) * 16 + t))
    return pairs


FIRST = torus_pairs("xy", 1), torus_pairs("xy", -1), torus_pairs("xy", 2)
SECOND = torus_pairs("yx", 1), torus_pairs("yx", -1), torus_pairs("yx", 2)


def turn_matrix():
    common = np.arange(BLOCK)[:, None] & np.arange(BLOCK)[None, :]
    parity = np.zeros((BLOCK, BLOCK), np.int64)
    for bit in range(BLOCK.bit_length() - 1):
        parity += (common >> bit) & 1
    return np.kron(np.eye(2), 1 - 2 * (parity % 2)).astype(np.float32)


def gather_matrix():
    row, column = np.arange(SHARE)[:, None], np.arange(BLOCK)[None, :]
    return (row // BLOCK == column).astype(np.float32)


def clipped_partial(pairs, signs, turn_ref, gather_ref):
    flat = jnp.concatenate(
        [
            (jnp.dot(rows, weight, preferred_element_type=jnp.float32) * signs).astype(jnp.bfloat16)
            for rows, weight in pairs
        ],
        0,
    )
    squares = jnp.dot(flat * flat, gather_ref[...], preferred_element_type=jnp.float32)
    limit = 2.0 * jnp.sqrt(squares + BLOCK * 1e-06)
    blocks = []
    for pair in range(2):
        columns = slice(pair * COLS, (pair + 1) * COLS)
        turned = jnp.dot(flat[:, columns], turn_ref[...], preferred_element_type=jnp.float32)
        for b in range(SUB):
            n = pair * SUB + b
            bound = jnp.broadcast_to(limit[:, n : n + 1], (2 * TOKENS, BLOCK))
            clipped = jnp.minimum(
                jnp.maximum(turned[:, b * BLOCK : (b + 1) * BLOCK], -bound), bound
            )
            blocks.append(clipped[:TOKENS] + clipped[TOKENS:])
    return blocks


GROUP = HEADS // 2 * TOKENS
LANES = KEY_BLOCK // 128


def attention_kernel(place_ref, query_hbm, held_ref, swapped_ref, o_ref, key, wide, scores, query_ref, sem):
    first, core, y, x = place_ref[0], place_ref[1], place_ref[3], place_ref[4]
    fetch = pltpu.make_async_copy(query_hbm, query_ref, sem)
    fetch.start()
    blocks = (first + TOKENS - 1) // KEY_BLOCK + 1
    gain = math.log2(math.e) / math.sqrt(HEAD)

    def sort(keys_ref, values_ref):
        @pl.loop(0, SIDE * SIDE)
        def _(n):
            far, near = (
                jnp.where(i == 1, SIDE - 1, jnp.maximum(i - 1, 0)) for i in (n // SIDE, lax.rem(n, SIDE))
            )
            block = pl.multiple_of(n * TOKENS, 32)
            row, column = lax.rem(y + far, SIDE), lax.rem(x + near, SIDE)
            start = pl.multiple_of((row * SIDE + column) * TOKENS, 32)
            key[pl.ds(start, TOKENS), :] = keys_ref[pl.ds(block, TOKENS), :]
            row, column = lax.rem(y + near, SIDE), lax.rem(x + far, SIDE)
            start = pl.multiple_of((row * SIDE + column) * TOKENS, 32)
            wide[pl.ds(start, TOKENS), :HEAD] = values_ref[pl.ds(block, TOKENS), :]

    @pl.when(core == 0)
    def _():
        sort(held_ref, swapped_ref)

    @pl.when(core != 0)
    def _():
        sort(swapped_ref, held_ref)

    wide[:, HEAD:] = jnp.ones((KEYS, HEAD), jnp.bfloat16)
    fetch.wait()
    whole = first // KEY_BLOCK
    query_pos = first + lax.rem(
        lax.broadcasted_iota(jnp.int32, (GROUP, 128), 0), TOKENS
    )
    key_pos = lax.broadcasted_iota(jnp.int32, (GROUP, 128), 1)
    rows = [
        jnp.concatenate([query_ref[:, h * HEAD : (h + 1) * HEAD] for h in (2 * g, 2 * g + 1)], 0)
        for g in range(2)
    ]

    def score(j, best, masked):
        start = pl.multiple_of(j * KEY_BLOCK, 128)
        result = []
        for group in range(2):
            part = lax.dot_general(
                rows[group],
                key[pl.ds(start, KEY_BLOCK), :],
                (((1,), (1,)), ((), ())),
                preferred_element_type=jnp.float32,
            )
            top = best[group]
            for t in range(LANES):
                piece = part[:, t * 128 : (t + 1) * 128]
                if masked:
                    piece = jnp.where(key_pos <= query_pos - (start + t * 128), piece, -1e30)
                scores[group, j, :, t * 128 : (t + 1) * 128] = piece
                top = jnp.maximum(top, piece)
            result.append(top)
        return tuple(result)

    low = jnp.full((GROUP, 128), -1e30, jnp.float32)

    best = lax.fori_loop(0, whole, lambda j, b: score(j, b, False), (low, low))
    best = lax.fori_loop(whole, blocks, lambda j, b: score(j, b, True), best)
    tops = [jnp.broadcast_to(jnp.max(b, axis=-1, keepdims=True), (GROUP, 128)) for b in best]

    def mix(j, totals):
        start = pl.multiple_of(j * KEY_BLOCK, 128)
        result = []
        for group in range(2):
            weights = jnp.concatenate(
                [
                    jnp.exp2((scores[group, j, :, t * 128 : (t + 1) * 128] - tops[group]) * gain).astype(
                        jnp.bfloat16
                    )
                    for t in range(LANES)
                ],
                1,
            )
            result.append(
                totals[group]
                + jnp.dot(
                    weights, wide[pl.ds(start, KEY_BLOCK), :], preferred_element_type=jnp.float32
                )
            )
        return tuple(result)

    none = jnp.zeros((GROUP, 2 * HEAD), jnp.float32)
    totals = lax.fori_loop(0, blocks, mix, (none, none))
    for group in range(2):
        normed = (totals[group][:, :HEAD] / totals[group][:, HEAD:]).astype(jnp.bfloat16)
        for h in range(2):
            column = (2 * group + h) * HEAD
            o_ref[:, column : column + HEAD] = normed[h * TOKENS : (h + 1) * TOKENS]


VMEM = pl.BlockSpec(memory_space=pltpu.VMEM)
SMEM = pl.BlockSpec(memory_space=pltpu.SMEM)
ANY = pl.BlockSpec(memory_space=pl.ANY)


HBM = pl.BlockSpec(memory_space=pltpu.HBM)


def attention(place, queries, held, swapped):
    return pl.pallas_call(
        attention_kernel,
        out_shape=jax.ShapeDtypeStruct((TOKENS, WIDTH), jnp.bfloat16),
        in_specs=[SMEM, HBM, VMEM, VMEM],
        out_specs=VMEM,
        scratch_shapes=[
            pltpu.VMEM((KEYS, HEAD), jnp.bfloat16),
            pltpu.VMEM((KEYS, 2 * HEAD), jnp.bfloat16),
            pltpu.VMEM((2, KEYS // KEY_BLOCK, GROUP, KEY_BLOCK), jnp.float32),
            pltpu.VMEM((TOKENS, WIDTH), jnp.bfloat16),
            pltpu.SemaphoreType.DMA,
        ],
        compiler_params=pltpu.CompilerParams(vmem_limit_bytes=30 << 20),
        cost_estimate=pl.CostEstimate(
            flops=8 * GROUP * KEYS * HEAD, bytes_accessed=3 << 20, transcendentals=2 * GROUP * KEYS
        ),
        name="attend",
    )(place, queries, held, swapped)


def project_kernel(
    place_ref, mine_ref, theirs_ref, own_hbm, other_hbm, sign_ref, turn_ref, gather_ref, *refs
):
    o_refs, (own, other, sems) = refs[: CHIPS + 1], refs[CHIPS + 1 :]
    core, chip, way = place_ref[1], place_ref[2], place_ref[5]

    def column(step):
        distance = 4 - (step + 1) // 2
        offset = way * jnp.where(lax.rem(step, 2) == 0, -distance, distance)
        return lax.rem(chip + offset + CHIPS, CHIPS) * CHUNK + core * SHARE

    def fetches(step):
        start = pl.multiple_of(column(step), SHARE)
        return [
            pltpu.make_async_copy(
                source.at[:, pl.ds(start, SHARE)], target.at[step], sems.at[n, step]
            )
            for n, (source, target) in enumerate(((own_hbm, own), (other_hbm, other)))
        ]

    @pl.loop(0, CHIPS)
    def _(step):
        for fetch in fetches(step):
            fetch.start()

    @pl.loop(0, CHIPS)
    def _(step):
        for fetch in fetches(step):
            fetch.wait()
        start = pl.multiple_of(column(step), SHARE)
        signs = (2 * sign_ref[:, pl.ds(start, SHARE)] - 1).astype(jnp.float32)
        blocks = clipped_partial(
            ((mine_ref[...], own[step]), (theirs_ref[...], other[step])), signs, turn_ref, gather_ref
        )
        for n in range(CHIPS):

            @pl.when(step == n)
            def _(n=n):
                for half in range(2):
                    o_ref, row = (o_refs[half], 0) if n == 0 else (o_refs[n + 1], half * ROWS)
                    for b in range(SUB):
                        piece = blocks[half * SUB + b]
                        o_ref[row + b * TOKENS : row + (b + 1) * TOKENS, :] = piece.astype(o_ref.dtype)


def project(place, mine, theirs, own, other, signs, turn, gatherer):
    half = jax.ShapeDtypeStruct((ROWS, BLOCK), jnp.bfloat16)
    both = jax.ShapeDtypeStruct((2 * ROWS, BLOCK), jnp.bfloat16)
    full = jax.ShapeDtypeStruct((2 * ROWS, BLOCK), jnp.float32)
    return pl.pallas_call(
        project_kernel,
        out_shape=(half,) * 2 + (both,) * (CHIPS - 2) + (full,),
        in_specs=[SMEM, VMEM, VMEM, HBM, HBM, VMEM, VMEM, VMEM],
        out_specs=(VMEM,) * (CHIPS + 1),
        scratch_shapes=[
            pltpu.VMEM((CHIPS, WIDTH, SHARE), jnp.bfloat16),
            pltpu.VMEM((CHIPS, WIDTH, SHARE), jnp.bfloat16),
            pltpu.SemaphoreType.DMA((2, CHIPS)),
        ],
        compiler_params=pltpu.CompilerParams(vmem_limit_bytes=50 << 20),
        cost_estimate=pl.CostEstimate(
            flops=2 * TOKENS * 1280 * D // 2, bytes_accessed=10 << 20, transcendentals=0
        ),
        name="project",
    )(place, mine, theirs, own, other, signs, turn, gatherer)


def pack_kernel(own, one, two, out, square):
    for half in range(2):
        lane = lax.broadcasted_iota(jnp.int32, (TOKENS, BLOCK), 1)
        columns = jnp.zeros((TOKENS, BLOCK), jnp.float32)
        for b in range(SUB):
            rows = slice(half * ROWS + b * TOKENS, half * ROWS + (b + 1) * TOKENS)
            came = one[rows, :].astype(jnp.float32) + two[rows, :].astype(jnp.float32)
            summed = (own[rows, :] + came) * (1.0 / math.sqrt(BLOCK))
            scale = jnp.max(jnp.abs(summed), axis=-1, keepdims=True) + 1e-06
            to = half * MSG + b * TOKENS
            out[to : to + TOKENS, :] = (summed / scale).astype(jnp.bfloat16)
            columns = jnp.where(lane == b, scale, columns)
        square[...] = jnp.zeros((2 * BLOCK, BLOCK), jnp.float32)
        square[:TOKENS, :] = columns
        turned = jnp.concatenate(
            [square[:BLOCK, :].T[:SUB, :], square[BLOCK:, :].T[:SUB, :]], 0
        )
        upper = turned.astype(jnp.bfloat16).astype(jnp.float32)
        tail = jnp.concatenate([upper, turned - upper, jnp.zeros((8, BLOCK), jnp.float32)], 0)
        out[half * MSG + ROWS : (half + 1) * MSG, :] = tail.astype(jnp.bfloat16)


def pack(own, one, two):
    return pl.pallas_call(
        pack_kernel,
        out_shape=jax.ShapeDtypeStruct((2 * MSG, BLOCK), jnp.bfloat16),
        in_specs=[VMEM] * 3,
        out_specs=VMEM,
        scratch_shapes=[pltpu.VMEM((2 * BLOCK, BLOCK), jnp.float32)],
        compiler_params=pltpu.CompilerParams(vmem_limit_bytes=8 << 20),
        cost_estimate=pl.CostEstimate(flops=1 << 20, bytes_accessed=1 << 20, transcendentals=0),
        name="pack",
    )(own, one, two)


def assemble_kernel(places, fresh, last, index_ref, *refs):
    count = 1 + max(place[0] for place in places)
    arrays, refs = refs[:count], refs[count:]
    if fresh:
        out_ref, table, tails, sems, tail_sems = refs
    else:
        _, old_table, out_ref, table, tails, sems, tail_sems = refs[:7]
        if last:
            _, _, out_ref, scale_ref, table, tails, sems, tail_sems = refs
        table[...] = old_table[...]
    core, chip, way = index_ref[1], index_ref[2], index_ref[5]

    def spot(swap, offset):
        side = (1 - core) if swap else core
        return side, lax.rem(chip + way * offset + CHIPS, CHIPS)

    copies, tail_copies = [], []
    for n, (array, row, swap, offset, half) in enumerate(places):
        tail_copies.append(
            pltpu.make_async_copy(
                arrays[array].at[pl.ds(row + ROWS, 16), :], tails.at[n], tail_sems.at[n]
            )
        )
        tail_copies[-1].start()
    for n, (array, row, swap, offset, half) in enumerate(places):
        side, place = spot(swap, offset)
        for b in range(SUB):
            column = pl.multiple_of(place * CHUNK + side * SHARE + half * COLS + b * BLOCK, BLOCK)
            copies.append(
                pltpu.make_async_copy(
                    arrays[array].at[pl.ds(row + b * TOKENS, TOKENS), :],
                    out_ref.at[:, pl.ds(column, BLOCK)],
                    sems.at[n * SUB + b],
                )
            )
            copies[-1].start()
    for n, (array, row, swap, offset, half) in enumerate(places):
        tail_copies[n].wait()
        side, place = spot(swap, offset)
        tail = tails[n].astype(jnp.float32)
        tail = tail[: 2 * SUB] + tail[2 * SUB : 4 * SUB]
        for t in range(2):
            table[place, side, half * SUB : (half + 1) * SUB, t * BLOCK : (t + 1) * BLOCK] = tail[
                t * SUB : (t + 1) * SUB
            ]
    if last:
        for place in range(CHIPS):
            for side in range(2):
                row = (2 * place + side) * 2 * SUB
                scale_ref[row : row + 2 * SUB, :] = table[place, side][:, :TOKENS]
    for copy in copies:
        copy.wait()


def assemble(index, arrays, places, before, last):
    table_shape = (CHIPS, 2, 2 * SUB, 2 * BLOCK)
    out_shape = [jax.ShapeDtypeStruct((TOKENS, D), jnp.bfloat16)]
    out_shape.append(
        jax.ShapeDtypeStruct((D // BLOCK, TOKENS) if last else table_shape, jnp.float32)
    )
    scratch = [pltpu.VMEM(table_shape, jnp.float32)] if last else []
    fresh = before is None
    return pl.pallas_call(
        functools.partial(assemble_kernel, places, fresh, last),
        out_shape=tuple(out_shape),
        in_specs=[SMEM] + [ANY] * len(arrays) + ([] if fresh else [ANY, VMEM]),
        out_specs=(ANY, VMEM),
        scratch_shapes=scratch
        + [
            pltpu.VMEM((len(places), 16, BLOCK), jnp.bfloat16),
            pltpu.SemaphoreType.DMA((len(places) * SUB,)),
            pltpu.SemaphoreType.DMA((len(places),)),
        ],
        input_output_aliases={} if fresh else {len(arrays) + 1: 0},
        compiler_params=pltpu.CompilerParams(vmem_limit_bytes=4 << 20),
        cost_estimate=pl.CostEstimate(flops=1 << 20, bytes_accessed=4 << 20, transcendentals=0),
        name="assemble",
    )(index, *arrays, *([] if fresh else before))


def add(arrived, own):
    return (arrived.astype(jnp.float32) + own.astype(jnp.float32)).astype(jnp.bfloat16)


def send(x, pairs):
    return lax.ppermute(x, "tp", pairs)


def layer(queries, keys, values, out_weight, signs):
    ctx, tp = lax.axis_index("ctx"), lax.axis_index("tp")
    core, chip = tp & 1, tp >> 1

    place = jnp.stack(
        [ctx * TOKENS, core, chip, ctx >> 2, ctx & 3, 1 - 2 * (chip & 1)]
    ).astype(jnp.int32)

    other_weight = send(out_weight, PAIR)

    def spread_out(x, pairs):
        came = [lax.ppermute(x, ("ctx", "tp"), way) for way in pairs]
        return jnp.concatenate([x, *came], 0)

    key_part = lax.dynamic_slice_in_dim(keys, chip * HEAD, HEAD, 1)
    value_part = lax.dynamic_slice_in_dim(values, chip * HEAD, HEAD, 1)
    held = spread_out(jnp.where(core == 0, key_part, value_part), FIRST)
    held = spread_out(held, SECOND)
    swapped = send(held, PAIR)

    turn = jnp.asarray(turn_matrix(), jnp.bfloat16)
    gatherer = jnp.asarray(gather_matrix(), jnp.bfloat16)
    attended = attention(place, queries, held, swapped)
    parts = project(
        place,
        attended,
        send(attended, PAIR),
        out_weight,
        other_weight,
        signs[None, :],
        turn,
        gatherer,
    )

    def exchange(for_a, for_b):
        came_b = send(for_a, WAY_A)
        came_a = send(for_b, WAY_B)
        return came_a, came_b

    came_a, came_b = exchange(parts[0], parts[1])
    for_a, for_b = parts[2], parts[3]
    for_a = lax.dynamic_update_slice(for_a, add(came_a, for_a[ROWS:]), (ROWS, 0))
    for_b = lax.dynamic_update_slice(for_b, add(came_b, for_b[:ROWS]), (0, 0))
    came_a, came_b = exchange(for_a, for_b)
    came_a, came_b = exchange(add(came_a, parts[4]), add(came_b, parts[5]))
    came_a, came_b = exchange(add(came_a, parts[6]), add(came_b, parts[7]))
    packed = pack(parts[8], came_a, came_b)

    stages = [[(packed, 0, None)]]
    came_a = came_b = packed
    for hop in range(1, 5):
        if hop < 4:
            came_a, came_b = exchange(came_a, came_b)
            stages.append([(came_a, -hop, None), (came_b, hop, None)])
        else:
            came_a, came_b = exchange(came_a[:MSG], came_b[MSG:])
            stages.append([(came_a, hop, 1), (came_b, hop, 0)])
    swapped_stages = []
    for stage in stages:
        swapped_stages.append([(send(array, PAIR), *rest) for array, *rest in stage])

    def gather(hops, before, last=False):
        arrays, places = [], []
        for swap, source in ((False, stages), (True, swapped_stages)):
            for hop in hops:
                for array, offset, half in source[hop]:
                    for h in (0, 1) if half is None else (half,):
                        row = h * MSG if half is None else 0
                        places.append((len(arrays), row, swap, offset, h))
                    arrays.append(array)
        return assemble(place, arrays, tuple(places), before, last)

    result = gather((0, 1), None)
    result = gather((2,), result)
    result = gather((3,), result)
    payload, scales = gather((4,), result, True)
    return payload, scales.T


def solution(mesh):
    return jax.shard_map(
        layer,
        mesh=mesh,
        in_specs=(P("ctx", "tp"), P("ctx", None), P("ctx", None), P("tp", None), P()),
        out_specs=(P("ctx", None), P("ctx", None)),
        check_vma=False,
    )
```

```python
import functools
import math

import jax
import jax.numpy as jnp
import numpy as np
from jax import lax
from jax.experimental import pallas as pl
from jax.experimental.pallas import tpu as pltpu
from jax.sharding import PartitionSpec as P


D = 8192
HEAD = 128
BLOCK = 128
CHIPS = 8
TOKENS = 224
HEADS = 4
WIDTH = HEADS * HEAD
KEYS = 3584
KEY_BLOCK = 896
CHUNK = D // CHIPS
SHARE = CHUNK // 2
COLS = SHARE // 2
SUB = COLS // BLOCK
ROWS = SUB * TOKENS
MSG = ROWS + 16

WAY_A = [(t, (t + 2 if t // 2 % 2 == 0 else t - 2) % 16) for t in range(16)]
WAY_B = [(t, (t - 2 if t // 2 % 2 == 0 else t + 2) % 16) for t in range(16)]
PAIR = [(t, t ^ 1) for t in range(16)]

SIDE = 4


def torus_pairs(axis_of_core, step):
    pairs = []
    for c in range(SIDE * SIDE):
        for t in range(16):
            y, x = divmod(c, SIDE)
            if axis_of_core[t % 2] == "x":
                x = (x + step) % SIDE
            else:
                y = (y + step) % SIDE
            pairs.append((c * 16 + t, (y * SIDE + x) * 16 + t))
    return pairs


FIRST = torus_pairs("xy", 1), torus_pairs("xy", -1), torus_pairs("xy", 2)
SECOND = torus_pairs("yx", 1), torus_pairs("yx", -1), torus_pairs("yx", 2)


def turn_matrix():
    common = np.arange(BLOCK)[:, None] & np.arange(BLOCK)[None, :]
    parity = np.zeros((BLOCK, BLOCK), np.int64)
    for bit in range(BLOCK.bit_length() - 1):
        parity += (common >> bit) & 1
    return np.kron(np.eye(2), 1 - 2 * (parity % 2)).astype(np.float32)


def gather_matrix():
    row, column = np.arange(SHARE)[:, None], np.arange(BLOCK)[None, :]
    return (row // BLOCK == column).astype(np.float32)


def clipped_partial(pairs, signs, turn_ref, gather_ref):
    flat = jnp.concatenate(
        [
            (jnp.dot(rows, weight, preferred_element_type=jnp.float32) * signs).astype(jnp.bfloat16)
            for rows, weight in pairs
        ],
        0,
    )
    squares = jnp.dot(flat * flat, gather_ref[...], preferred_element_type=jnp.float32)
    limit = 2.0 * jnp.sqrt(squares + BLOCK * 1e-06)
    blocks = []
    for pair in range(2):
        columns = slice(pair * COLS, (pair + 1) * COLS)
        turned = jnp.dot(flat[:, columns], turn_ref[...], preferred_element_type=jnp.float32)
        for b in range(SUB):
            n = pair * SUB + b
            bound = jnp.broadcast_to(limit[:, n : n + 1], (2 * TOKENS, BLOCK))
            clipped = jnp.minimum(
                jnp.maximum(turned[:, b * BLOCK : (b + 1) * BLOCK], -bound), bound
            )
            blocks.append(clipped[:TOKENS] + clipped[TOKENS:])
    return blocks


GROUP = HEADS // 2 * TOKENS
LANES = KEY_BLOCK // 128


def attention_kernel(place_ref, query_hbm, held_ref, swapped_ref, o_ref, key, wide, scores, query_ref, sem):
    first, core, y, x = place_ref[0], place_ref[1], place_ref[3], place_ref[4]
    fetch = pltpu.make_async_copy(query_hbm, query_ref, sem)
    fetch.start()
    blocks = (first + TOKENS - 1) // KEY_BLOCK + 1
    gain = math.log2(math.e) / math.sqrt(HEAD)

    def sort(keys_ref, values_ref):
        @pl.loop(0, SIDE * SIDE)
        def _(n):
            far, near = (
                jnp.where(i == 1, SIDE - 1, jnp.maximum(i - 1, 0)) for i in (n // SIDE, lax.rem(n, SIDE))
            )
            block = pl.multiple_of(n * TOKENS, 32)
            row, column = lax.rem(y + far, SIDE), lax.rem(x + near, SIDE)
            start = pl.multiple_of((row * SIDE + column) * TOKENS, 32)
            key[pl.ds(start, TOKENS), :] = keys_ref[pl.ds(block, TOKENS), :]
            row, column = lax.rem(y + near, SIDE), lax.rem(x + far, SIDE)
            start = pl.multiple_of((row * SIDE + column) * TOKENS, 32)
            wide[pl.ds(start, TOKENS), :HEAD] = values_ref[pl.ds(block, TOKENS), :]

    @pl.when(core == 0)
    def _():
        sort(held_ref, swapped_ref)

    @pl.when(core != 0)
    def _():
        sort(swapped_ref, held_ref)

    wide[:, HEAD:] = jnp.ones((KEYS, HEAD), jnp.bfloat16)
    fetch.wait()
    whole = first // KEY_BLOCK
    query_pos = first + lax.rem(
        lax.broadcasted_iota(jnp.int32, (GROUP, 128), 0), TOKENS
    )
    key_pos = lax.broadcasted_iota(jnp.int32, (GROUP, 128), 1)
    rows = [
        jnp.concatenate([query_ref[:, h * HEAD : (h + 1) * HEAD] for h in (2 * g, 2 * g + 1)], 0)
        for g in range(2)
    ]

    def score(j, best, masked):
        start = pl.multiple_of(j * KEY_BLOCK, 128)
        result = []
        for group in range(2):
            part = lax.dot_general(
                rows[group],
                key[pl.ds(start, KEY_BLOCK), :],
                (((1,), (1,)), ((), ())),
                preferred_element_type=jnp.float32,
            )
            top = best[group]
            for t in range(LANES):
                piece = part[:, t * 128 : (t + 1) * 128]
                if masked:
                    piece = jnp.where(key_pos <= query_pos - (start + t * 128), piece, -1e30)
                scores[group, j, :, t * 128 : (t + 1) * 128] = piece
                top = jnp.maximum(top, piece)
            result.append(top)
        return tuple(result)

    low = jnp.full((GROUP, 128), -1e30, jnp.float32)

    best = lax.fori_loop(0, whole, lambda j, b: score(j, b, False), (low, low))
    best = lax.fori_loop(whole, blocks, lambda j, b: score(j, b, True), best)
    tops = [jnp.broadcast_to(jnp.max(b, axis=-1, keepdims=True), (GROUP, 128)) for b in best]

    def mix(j, totals):
        start = pl.multiple_of(j * KEY_BLOCK, 128)
        result = []
        for group in range(2):
            weights = jnp.concatenate(
                [
                    jnp.exp2((scores[group, j, :, t * 128 : (t + 1) * 128] - tops[group]) * gain).astype(
                        jnp.bfloat16
                    )
                    for t in range(LANES)
                ],
                1,
            )
            result.append(
                totals[group]
                + jnp.dot(
                    weights, wide[pl.ds(start, KEY_BLOCK), :], preferred_element_type=jnp.float32
                )
            )
        return tuple(result)

    none = jnp.zeros((GROUP, 2 * HEAD), jnp.float32)
    totals = lax.fori_loop(0, blocks, mix, (none, none))
    for group in range(2):
        normed = (totals[group][:, :HEAD] / totals[group][:, HEAD:]).astype(jnp.bfloat16)
        for h in range(2):
            column = (2 * group + h) * HEAD
            o_ref[:, column : column + HEAD] = normed[h * TOKENS : (h + 1) * TOKENS]


VMEM = pl.BlockSpec(memory_space=pltpu.VMEM)
SMEM = pl.BlockSpec(memory_space=pltpu.SMEM)
ANY = pl.BlockSpec(memory_space=pl.ANY)


HBM = pl.BlockSpec(memory_space=pltpu.HBM)


def attention(place, queries, held, swapped):
    return pl.pallas_call(
        attention_kernel,
        out_shape=jax.ShapeDtypeStruct((TOKENS, WIDTH), jnp.bfloat16),
        in_specs=[SMEM, HBM, VMEM, VMEM],
        out_specs=VMEM,
        scratch_shapes=[
            pltpu.VMEM((KEYS, HEAD), jnp.bfloat16),
            pltpu.VMEM((KEYS, 2 * HEAD), jnp.bfloat16),
            pltpu.VMEM((2, KEYS // KEY_BLOCK, GROUP, KEY_BLOCK), jnp.float32),
            pltpu.VMEM((TOKENS, WIDTH), jnp.bfloat16),
            pltpu.SemaphoreType.DMA,
        ],
        compiler_params=pltpu.CompilerParams(vmem_limit_bytes=30 << 20),
        cost_estimate=pl.CostEstimate(
            flops=8 * GROUP * KEYS * HEAD, bytes_accessed=3 << 20, transcendentals=2 * GROUP * KEYS
        ),
        name="attend",
    )(place, queries, held, swapped)


def project_kernel(
    place_ref, mine_ref, theirs_ref, own_hbm, other_hbm, sign_ref, turn_ref, gather_ref, *refs
):
    o_refs, (own, other, sems) = refs[: 2 * CHIPS - 1], refs[2 * CHIPS - 1 :]
    core, chip, way = place_ref[1], place_ref[2], place_ref[5]

    def column(step):
        distance = 4 - (step + 1) // 2
        offset = way * jnp.where(lax.rem(step, 2) == 0, -distance, distance)
        return lax.rem(chip + offset + CHIPS, CHIPS) * CHUNK + core * SHARE

    def fetches(step):
        start = pl.multiple_of(column(step), SHARE)
        return [
            pltpu.make_async_copy(
                source.at[:, pl.ds(start, SHARE)], target.at[step], sems.at[n, step]
            )
            for n, (source, target) in enumerate(((own_hbm, own), (other_hbm, other)))
        ]

    @pl.loop(0, CHIPS)
    def _(step):
        for fetch in fetches(step):
            fetch.start()

    @pl.loop(0, CHIPS)
    def _(step):
        for fetch in fetches(step):
            fetch.wait()
        start = pl.multiple_of(column(step), SHARE)
        signs = (2 * sign_ref[:, pl.ds(start, SHARE)] - 1).astype(jnp.float32)
        blocks = clipped_partial(
            ((mine_ref[...], own[step]), (theirs_ref[...], other[step])), signs, turn_ref, gather_ref
        )
        for n in range(CHIPS):

            @pl.when(step == n)
            def _(n=n):
                for half in range(2):
                    o_ref, row = (o_refs[2 * n + half], 0) if n < CHIPS - 1 else (o_refs[2 * n], half * ROWS)
                    for b in range(SUB):
                        piece = blocks[half * SUB + b]
                        o_ref[row + b * TOKENS : row + (b + 1) * TOKENS, :] = piece.astype(o_ref.dtype)


def project(place, mine, theirs, own, other, signs, turn, gatherer):
    half = jax.ShapeDtypeStruct((ROWS, BLOCK), jnp.bfloat16)
    full = jax.ShapeDtypeStruct((2 * ROWS, BLOCK), jnp.float32)
    return pl.pallas_call(
        project_kernel,
        out_shape=(half,) * (2 * CHIPS - 2) + (full,),
        in_specs=[SMEM, VMEM, VMEM, HBM, HBM, VMEM, VMEM, VMEM],
        out_specs=(VMEM,) * (2 * CHIPS - 1),
        scratch_shapes=[
            pltpu.VMEM((CHIPS, WIDTH, SHARE), jnp.bfloat16),
            pltpu.VMEM((CHIPS, WIDTH, SHARE), jnp.bfloat16),
            pltpu.SemaphoreType.DMA((2, CHIPS)),
        ],
        compiler_params=pltpu.CompilerParams(vmem_limit_bytes=50 << 20),
        cost_estimate=pl.CostEstimate(
            flops=2 * TOKENS * 1280 * D // 2, bytes_accessed=10 << 20, transcendentals=0
        ),
        name="project",
    )(place, mine, theirs, own, other, signs, turn, gatherer)


def pack_kernel(own, one0, two0, one1, two1, out0, out1, square):
    for half, (one, two, out) in enumerate(((one0, two0, out0), (one1, two1, out1))):
        lane = lax.broadcasted_iota(jnp.int32, (TOKENS, BLOCK), 1)
        columns = jnp.zeros((TOKENS, BLOCK), jnp.float32)
        for b in range(SUB):
            rows = slice(b * TOKENS, (b + 1) * TOKENS)
            came = one[rows, :].astype(jnp.float32) + two[rows, :].astype(jnp.float32)
            summed = (own[half * ROWS + b * TOKENS : half * ROWS + (b + 1) * TOKENS, :] + came) * (1.0 / math.sqrt(BLOCK))
            scale = jnp.max(jnp.abs(summed), axis=-1, keepdims=True) + 1e-06
            out[rows, :] = (summed / scale).astype(jnp.bfloat16)
            columns = jnp.where(lane == b, scale, columns)
        square[...] = jnp.zeros((2 * BLOCK, BLOCK), jnp.float32)
        square[:TOKENS, :] = columns
        turned = jnp.concatenate(
            [square[:BLOCK, :].T[:SUB, :], square[BLOCK:, :].T[:SUB, :]], 0
        )
        upper = turned.astype(jnp.bfloat16).astype(jnp.float32)
        tail = jnp.concatenate([upper, turned - upper, jnp.zeros((8, BLOCK), jnp.float32)], 0)
        out[ROWS:, :] = tail.astype(jnp.bfloat16)


def pack(own, first, second):
    shape = jax.ShapeDtypeStruct((MSG, BLOCK), jnp.bfloat16)
    return pl.pallas_call(
        pack_kernel,
        out_shape=(shape, shape),
        in_specs=[VMEM] * 5,
        out_specs=(VMEM, VMEM),
        scratch_shapes=[pltpu.VMEM((2 * BLOCK, BLOCK), jnp.float32)],
        compiler_params=pltpu.CompilerParams(vmem_limit_bytes=8 << 20),
        cost_estimate=pl.CostEstimate(flops=1 << 20, bytes_accessed=1 << 20, transcendentals=0),
        name="pack",
    )(own, *first, *second)


def assemble_kernel(places, fresh, last, index_ref, *refs):
    count = 1 + max(place[0] for place in places)
    arrays, refs = refs[:count], refs[count:]
    if fresh:
        out_ref, table, tails, sems, tail_sems = refs
    else:
        _, old_table, out_ref, table, tails, sems, tail_sems = refs[:7]
        if last:
            _, _, out_ref, scale_ref, table, tails, sems, tail_sems = refs
        table[...] = old_table[...]
    core, chip, way = index_ref[1], index_ref[2], index_ref[5]

    def spot(swap, offset):
        side = (1 - core) if swap else core
        return side, lax.rem(chip + way * offset + CHIPS, CHIPS)

    copies, tail_copies = [], []
    for n, (array, row, swap, offset, half) in enumerate(places):
        tail_copies.append(
            pltpu.make_async_copy(
                arrays[array].at[pl.ds(row + ROWS, 16), :], tails.at[n], tail_sems.at[n]
            )
        )
        tail_copies[-1].start()
    for n, (array, row, swap, offset, half) in enumerate(places):
        side, place = spot(swap, offset)
        for b in range(SUB):
            column = pl.multiple_of(place * CHUNK + side * SHARE + half * COLS + b * BLOCK, BLOCK)
            copies.append(
                pltpu.make_async_copy(
                    arrays[array].at[pl.ds(row + b * TOKENS, TOKENS), :],
                    out_ref.at[:, pl.ds(column, BLOCK)],
                    sems.at[n * SUB + b],
                )
            )
            copies[-1].start()
    for n, (array, row, swap, offset, half) in enumerate(places):
        tail_copies[n].wait()
        side, place = spot(swap, offset)
        tail = tails[n].astype(jnp.float32)
        tail = tail[: 2 * SUB] + tail[2 * SUB : 4 * SUB]
        for t in range(2):
            table[place, side, half * SUB : (half + 1) * SUB, t * BLOCK : (t + 1) * BLOCK] = tail[
                t * SUB : (t + 1) * SUB
            ]
    if last:
        for place in range(CHIPS):
            for side in range(2):
                row = (2 * place + side) * 2 * SUB
                scale_ref[row : row + 2 * SUB, :] = table[place, side][:, :TOKENS]
    for copy in copies:
        copy.wait()


def assemble(index, arrays, places, before, last):
    table_shape = (CHIPS, 2, 2 * SUB, 2 * BLOCK)
    out_shape = [jax.ShapeDtypeStruct((TOKENS, D), jnp.bfloat16)]
    out_shape.append(
        jax.ShapeDtypeStruct((D // BLOCK, TOKENS) if last else table_shape, jnp.float32)
    )
    scratch = [pltpu.VMEM(table_shape, jnp.float32)] if last else []
    fresh = before is None
    return pl.pallas_call(
        functools.partial(assemble_kernel, places, fresh, last),
        out_shape=tuple(out_shape),
        in_specs=[SMEM] + [ANY] * len(arrays) + ([] if fresh else [ANY, VMEM]),
        out_specs=(ANY, VMEM),
        scratch_shapes=scratch
        + [
            pltpu.VMEM((len(places), 16, BLOCK), jnp.bfloat16),
            pltpu.SemaphoreType.DMA((len(places) * SUB,)),
            pltpu.SemaphoreType.DMA((len(places),)),
        ],
        input_output_aliases={} if fresh else {len(arrays) + 1: 0},
        compiler_params=pltpu.CompilerParams(vmem_limit_bytes=4 << 20),
        cost_estimate=pl.CostEstimate(flops=1 << 20, bytes_accessed=4 << 20, transcendentals=0),
        name="assemble",
    )(index, *arrays, *([] if fresh else before))


def add(arrived, own):
    return (arrived.astype(jnp.float32) + own.astype(jnp.float32)).astype(jnp.bfloat16)


def send(x, pairs):
    return lax.ppermute(x, "tp", pairs)


def layer(queries, keys, values, out_weight, signs):
    ctx, tp = lax.axis_index("ctx"), lax.axis_index("tp")
    core, chip = tp & 1, tp >> 1

    place = jnp.stack(
        [ctx * TOKENS, core, chip, ctx >> 2, ctx & 3, 1 - 2 * (chip & 1)]
    ).astype(jnp.int32)

    other_weight = send(out_weight, PAIR)

    def spread_out(x, pairs):
        came = [lax.ppermute(x, ("ctx", "tp"), way) for way in pairs]
        return jnp.concatenate([x, *came], 0)

    key_part = lax.dynamic_slice_in_dim(keys, chip * HEAD, HEAD, 1)
    value_part = lax.dynamic_slice_in_dim(values, chip * HEAD, HEAD, 1)
    held = spread_out(jnp.where(core == 0, key_part, value_part), FIRST)
    held = spread_out(held, SECOND)
    swapped = send(held, PAIR)

    turn = jnp.asarray(turn_matrix(), jnp.bfloat16)
    gatherer = jnp.asarray(gather_matrix(), jnp.bfloat16)
    attended = attention(place, queries, held, swapped)
    parts = project(
        place,
        attended,
        send(attended, PAIR),
        out_weight,
        other_weight,
        signs[None, :],
        turn,
        gatherer,
    )

    def exchange(for_a, for_b):
        came_b = send(for_a, WAY_A)
        came_a = send(for_b, WAY_B)
        return came_a, came_b

    def part(distance, way, half):
        return parts[half if distance == 4 else 2 + 4 * (3 - distance) + 2 * way + half]

    came = {}
    for step, (distance, half) in enumerate(((4, 0), (3, 0), (3, 1), (2, 1), (2, 0), (1, 0), (1, 1))):
        for_a, for_b = part(distance, 0, half), part(distance, 1, 1 - half)
        if step >= 2:
            came_a, came_b = lax.optimization_barrier(came[step - 2])
            for_a, for_b = add(came_a, for_a), add(came_b, for_b)
        came[step] = exchange(for_a, for_b)
    packed = pack(parts[14], (came[6][0], came[5][1]), (came[5][0], came[6][1]))

    steps, place_of = [], []
    sends = [((packed[0], 0), (packed[1], 1)), ((packed[1], 1), (packed[0], 0))]
    for step in range(7):
        (for_a, half_a), (for_b, half_b) = sends[step]
        for_a, for_b = lax.optimization_barrier((for_a, for_b))
        came_a, came_b = exchange(for_a, for_b)
        sends.append(((came_a, half_b), (came_b, half_a)))
        hop = step // 2 + 1
        steps.append((came_a, came_b))
        place_of.append(((-hop, half_b), (hop, half_a)))
    steps.insert(0, tuple(packed))
    place_of.insert(0, ((0, 0), (0, 1)))
    swapped = []
    for pieces in steps:
        joined = jnp.concatenate(pieces, 0)
        swapped.append(send(joined, PAIR))

    def gather(which, before, last=False):
        arrays, places = [], []
        for step in which:
            for piece, spot in zip(steps[step], place_of[step]):
                places.append((len(arrays), 0, False, *spot))
                arrays.append(piece)
        for step in which:
            for row, spot in zip((0, MSG), place_of[step]):
                places.append((len(arrays), row, True, *spot))
            arrays.append(swapped[step])
        return assemble(place, arrays, tuple(places), before, last)

    result = gather((0, 1, 2), None)
    result = gather((3, 4), result)
    result = gather((5, 6), result)
    payload, scales = gather((7,), result, True)
    return payload, scales.T


def solution(mesh):
    return jax.shard_map(
        layer,
        mesh=mesh,
        in_specs=(P("ctx", "tp"), P("ctx", None), P("ctx", None), P("tp", None), P()),
        out_specs=(P("ctx", None), P("ctx", None)),
        check_vma=False,
    )
```

```python
import functools
import math

import jax
import jax.numpy as jnp
import numpy as np
from jax import lax
from jax.experimental import pallas as pl
from jax.experimental.pallas import tpu as pltpu
from jax.sharding import PartitionSpec as P


D = 8192
HEAD = 128
BLOCK = 128
CHIPS = 8
TOKENS = 224
HEADS = 4
WIDTH = HEADS * HEAD
KEYS = 3584
KEY_BLOCK = 896
CHUNK = D // CHIPS
SHARE = CHUNK // 2
COLS = SHARE // 2
SUB = COLS // BLOCK
ROWS = SUB * TOKENS
MSG = ROWS + 16

WAY_A = [(t, (t + 2 if t // 2 % 2 == 0 else t - 2) % 16) for t in range(16)]
WAY_B = [(t, (t - 2 if t // 2 % 2 == 0 else t + 2) % 16) for t in range(16)]
PAIR = [(t, t ^ 1) for t in range(16)]

SIDE = 4


def torus_pairs(axis_of_core, step):
    pairs = []
    for c in range(SIDE * SIDE):
        for t in range(16):
            y, x = divmod(c, SIDE)
            if axis_of_core[t % 2] == "x":
                x = (x + step) % SIDE
            else:
                y = (y + step) % SIDE
            pairs.append((c * 16 + t, (y * SIDE + x) * 16 + t))
    return pairs


FIRST = torus_pairs("xy", 1), torus_pairs("xy", -1), torus_pairs("xy", 2)
SECOND = torus_pairs("yx", 1), torus_pairs("yx", -1), torus_pairs("yx", 2)


def turn_matrix():
    common = np.arange(BLOCK)[:, None] & np.arange(BLOCK)[None, :]
    parity = np.zeros((BLOCK, BLOCK), np.int64)
    for bit in range(BLOCK.bit_length() - 1):
        parity += (common >> bit) & 1
    return np.kron(np.eye(2), 1 - 2 * (parity % 2)).astype(np.float32)


def gather_matrix():
    row, column = np.arange(SHARE)[:, None], np.arange(BLOCK)[None, :]
    return (row // BLOCK == column).astype(np.float32)


def clipped_partial(pairs, signs, turn_ref, gather_ref):
    flat = jnp.concatenate(
        [
            (jnp.dot(rows, weight, preferred_element_type=jnp.float32) * signs).astype(jnp.bfloat16)
            for rows, weight in pairs
        ],
        0,
    )
    squares = jnp.dot(flat * flat, gather_ref[...], preferred_element_type=jnp.float32)
    limit = 2.0 * jnp.sqrt(squares + BLOCK * 1e-06)
    blocks = []
    for pair in range(2):
        columns = slice(pair * COLS, (pair + 1) * COLS)
        turned = jnp.dot(flat[:, columns], turn_ref[...], preferred_element_type=jnp.float32)
        for b in range(SUB):
            n = pair * SUB + b
            bound = jnp.broadcast_to(limit[:, n : n + 1], (2 * TOKENS, BLOCK))
            clipped = jnp.minimum(
                jnp.maximum(turned[:, b * BLOCK : (b + 1) * BLOCK], -bound), bound
            )
            blocks.append(clipped[:TOKENS] + clipped[TOKENS:])
    return blocks


GROUP = HEADS // 2 * TOKENS
LANES = KEY_BLOCK // 128


def attention_kernel(place_ref, query_hbm, held_ref, swapped_ref, o_ref, key, wide, scores, query_ref, sem):
    first, core, y, x = place_ref[0], place_ref[1], place_ref[3], place_ref[4]
    fetch = pltpu.make_async_copy(query_hbm, query_ref, sem)
    fetch.start()
    blocks = (first + TOKENS - 1) // KEY_BLOCK + 1
    gain = math.log2(math.e) / math.sqrt(HEAD)

    def sort(keys_ref, values_ref):
        @pl.loop(0, SIDE * SIDE)
        def _(n):
            far, near = (
                jnp.where(i == 1, SIDE - 1, jnp.maximum(i - 1, 0)) for i in (n // SIDE, lax.rem(n, SIDE))
            )
            block = pl.multiple_of(n * TOKENS, 32)
            row, column = lax.rem(y + far, SIDE), lax.rem(x + near, SIDE)
            start = pl.multiple_of((row * SIDE + column) * TOKENS, 32)
            key[pl.ds(start, TOKENS), :] = keys_ref[pl.ds(block, TOKENS), :]
            row, column = lax.rem(y + near, SIDE), lax.rem(x + far, SIDE)
            start = pl.multiple_of((row * SIDE + column) * TOKENS, 32)
            wide[pl.ds(start, TOKENS), :HEAD] = values_ref[pl.ds(block, TOKENS), :]

    @pl.when(core == 0)
    def _():
        sort(held_ref, swapped_ref)

    @pl.when(core != 0)
    def _():
        sort(swapped_ref, held_ref)

    wide[:, HEAD:] = jnp.ones((KEYS, HEAD), jnp.bfloat16)
    fetch.wait()
    whole = first // KEY_BLOCK
    query_pos = first + lax.rem(
        lax.broadcasted_iota(jnp.int32, (GROUP, 128), 0), TOKENS
    )
    key_pos = lax.broadcasted_iota(jnp.int32, (GROUP, 128), 1)
    rows = [
        jnp.concatenate([query_ref[:, h * HEAD : (h + 1) * HEAD] for h in (2 * g, 2 * g + 1)], 0)
        for g in range(2)
    ]

    def score(j, best, masked):
        start = pl.multiple_of(j * KEY_BLOCK, 128)
        result = []
        for group in range(2):
            part = lax.dot_general(
                rows[group],
                key[pl.ds(start, KEY_BLOCK), :],
                (((1,), (1,)), ((), ())),
                preferred_element_type=jnp.float32,
            )
            top = best[group]
            for t in range(LANES):
                piece = part[:, t * 128 : (t + 1) * 128]
                if masked:
                    piece = jnp.where(key_pos <= query_pos - (start + t * 128), piece, -1e30)
                scores[group, j, :, t * 128 : (t + 1) * 128] = piece
                top = jnp.maximum(top, piece)
            result.append(top)
        return tuple(result)

    low = jnp.full((GROUP, 128), -1e30, jnp.float32)

    best = lax.fori_loop(0, whole, lambda j, b: score(j, b, False), (low, low))
    best = lax.fori_loop(whole, blocks, lambda j, b: score(j, b, True), best)
    tops = [jnp.broadcast_to(jnp.max(b, axis=-1, keepdims=True), (GROUP, 128)) for b in best]

    def mix(j, totals):
        start = pl.multiple_of(j * KEY_BLOCK, 128)
        result = []
        for group in range(2):
            weights = jnp.concatenate(
                [
                    jnp.exp2((scores[group, j, :, t * 128 : (t + 1) * 128] - tops[group]) * gain).astype(
                        jnp.bfloat16
                    )
                    for t in range(LANES)
                ],
                1,
            )
            result.append(
                totals[group]
                + jnp.dot(
                    weights, wide[pl.ds(start, KEY_BLOCK), :], preferred_element_type=jnp.float32
                )
            )
        return tuple(result)

    none = jnp.zeros((GROUP, 2 * HEAD), jnp.float32)
    totals = lax.fori_loop(0, blocks, mix, (none, none))
    for group in range(2):
        normed = (totals[group][:, :HEAD] / totals[group][:, HEAD:]).astype(jnp.bfloat16)
        for h in range(2):
            column = (2 * group + h) * HEAD
            o_ref[:, column : column + HEAD] = normed[h * TOKENS : (h + 1) * TOKENS]


VMEM = pl.BlockSpec(memory_space=pltpu.VMEM)
SMEM = pl.BlockSpec(memory_space=pltpu.SMEM)
ANY = pl.BlockSpec(memory_space=pl.ANY)


HBM = pl.BlockSpec(memory_space=pltpu.HBM)


def attention(place, queries, held, swapped):
    return pl.pallas_call(
        attention_kernel,
        out_shape=jax.ShapeDtypeStruct((TOKENS, WIDTH), jnp.bfloat16),
        in_specs=[SMEM, HBM, VMEM, VMEM],
        out_specs=VMEM,
        scratch_shapes=[
            pltpu.VMEM((KEYS, HEAD), jnp.bfloat16),
            pltpu.VMEM((KEYS, 2 * HEAD), jnp.bfloat16),
            pltpu.VMEM((2, KEYS // KEY_BLOCK, GROUP, KEY_BLOCK), jnp.float32),
            pltpu.VMEM((TOKENS, WIDTH), jnp.bfloat16),
            pltpu.SemaphoreType.DMA,
        ],
        compiler_params=pltpu.CompilerParams(vmem_limit_bytes=30 << 20),
        cost_estimate=pl.CostEstimate(
            flops=8 * GROUP * KEYS * HEAD, bytes_accessed=3 << 20, transcendentals=2 * GROUP * KEYS
        ),
        name="attend",
    )(place, queries, held, swapped)


def project_kernel(
    place_ref, mine_ref, theirs_ref, own_hbm, other_hbm, sign_ref, turn_ref, gather_ref, *refs
):
    o_refs, (own, other, sems) = refs[: 2 * CHIPS - 1], refs[2 * CHIPS - 1 :]
    core, chip, way = place_ref[1], place_ref[2], place_ref[5]

    def column(step):
        distance = 4 - (step + 1) // 2
        offset = way * jnp.where(lax.rem(step, 2) == 0, -distance, distance)
        return lax.rem(chip + offset + CHIPS, CHIPS) * CHUNK + core * SHARE

    def fetches(step):
        start = pl.multiple_of(column(step), SHARE)
        return [
            pltpu.make_async_copy(
                source.at[:, pl.ds(start, SHARE)], target.at[step], sems.at[n, step]
            )
            for n, (source, target) in enumerate(((own_hbm, own), (other_hbm, other)))
        ]

    @pl.loop(0, CHIPS)
    def _(step):
        for fetch in fetches(step):
            fetch.start()

    @pl.loop(0, CHIPS)
    def _(step):
        for fetch in fetches(step):
            fetch.wait()
        start = pl.multiple_of(column(step), SHARE)
        signs = (2 * sign_ref[:, pl.ds(start, SHARE)] - 1).astype(jnp.float32)
        blocks = clipped_partial(
            ((mine_ref[...], own[step]), (theirs_ref[...], other[step])), signs, turn_ref, gather_ref
        )
        for n in range(CHIPS):

            @pl.when(step == n)
            def _(n=n):
                for half in range(2):
                    o_ref, row = (o_refs[2 * n + half], 0) if n < CHIPS - 1 else (o_refs[2 * n], half * ROWS)
                    for b in range(SUB):
                        piece = blocks[half * SUB + b]
                        o_ref[row + b * TOKENS : row + (b + 1) * TOKENS, :] = piece.astype(o_ref.dtype)


def project(place, mine, theirs, own, other, signs, turn, gatherer):
    half = jax.ShapeDtypeStruct((ROWS, BLOCK), jnp.bfloat16)
    full = jax.ShapeDtypeStruct((2 * ROWS, BLOCK), jnp.float32)
    return pl.pallas_call(
        project_kernel,
        out_shape=(half,) * (2 * CHIPS - 2) + (full,),
        in_specs=[SMEM, VMEM, VMEM, HBM, HBM, VMEM, VMEM, VMEM],
        out_specs=(VMEM,) * (2 * CHIPS - 1),
        scratch_shapes=[
            pltpu.VMEM((CHIPS, WIDTH, SHARE), jnp.bfloat16),
            pltpu.VMEM((CHIPS, WIDTH, SHARE), jnp.bfloat16),
            pltpu.SemaphoreType.DMA((2, CHIPS)),
        ],
        compiler_params=pltpu.CompilerParams(vmem_limit_bytes=50 << 20),
        cost_estimate=pl.CostEstimate(
            flops=2 * TOKENS * 1280 * D // 2, bytes_accessed=10 << 20, transcendentals=0
        ),
        name="project",
    )(place, mine, theirs, own, other, signs, turn, gatherer)


def pack_kernel(own, one0, two0, one1, two1, out0, out1, square):
    for half, (one, two, out) in enumerate(((one0, two0, out0), (one1, two1, out1))):
        lane = lax.broadcasted_iota(jnp.int32, (TOKENS, BLOCK), 1)
        columns = jnp.zeros((TOKENS, BLOCK), jnp.float32)
        for b in range(SUB):
            rows = slice(b * TOKENS, (b + 1) * TOKENS)
            came = one[rows, :].astype(jnp.float32) + two[rows, :].astype(jnp.float32)
            summed = (own[half * ROWS + b * TOKENS : half * ROWS + (b + 1) * TOKENS, :] + came) * (1.0 / math.sqrt(BLOCK))
            scale = jnp.max(jnp.abs(summed), axis=-1, keepdims=True) + 1e-06
            out[rows, :] = (summed / scale).astype(jnp.bfloat16)
            columns = jnp.where(lane == b, scale, columns)
        square[...] = jnp.zeros((2 * BLOCK, BLOCK), jnp.float32)
        square[:TOKENS, :] = columns
        turned = jnp.concatenate(
            [square[:BLOCK, :].T[:SUB, :], square[BLOCK:, :].T[:SUB, :]], 0
        )
        upper = turned.astype(jnp.bfloat16).astype(jnp.float32)
        tail = jnp.concatenate([upper, turned - upper, jnp.zeros((8, BLOCK), jnp.float32)], 0)
        out[ROWS:, :] = tail.astype(jnp.bfloat16)


def pack(own, first, second):
    shape = jax.ShapeDtypeStruct((MSG, BLOCK), jnp.bfloat16)
    return pl.pallas_call(
        pack_kernel,
        out_shape=(shape, shape),
        in_specs=[VMEM] * 5,
        out_specs=(VMEM, VMEM),
        scratch_shapes=[pltpu.VMEM((2 * BLOCK, BLOCK), jnp.float32)],
        compiler_params=pltpu.CompilerParams(vmem_limit_bytes=8 << 20),
        cost_estimate=pl.CostEstimate(flops=1 << 20, bytes_accessed=1 << 20, transcendentals=0),
        name="pack",
    )(own, *first, *second)


def assemble_kernel(places, fresh, last, index_ref, *refs):
    count = 1 + max(place[0] for place in places)
    arrays, refs = refs[:count], refs[count:]
    if fresh:
        out_ref, table, tails, sems, tail_sems = refs
    else:
        _, old_table, out_ref, table, tails, sems, tail_sems = refs[:7]
        if last:
            _, _, out_ref, scale_ref, table, tails, sems, tail_sems = refs
        table[...] = old_table[...]
    core, chip, way = index_ref[1], index_ref[2], index_ref[5]

    def spot(swap, offset):
        side = (1 - core) if swap else core
        return side, lax.rem(chip + way * offset + CHIPS, CHIPS)

    copies, tail_copies = [], []
    for n, (array, row, swap, offset, half) in enumerate(places):
        tail_copies.append(
            pltpu.make_async_copy(
                arrays[array].at[pl.ds(row + ROWS, 16), :], tails.at[n], tail_sems.at[n]
            )
        )
        tail_copies[-1].start()
    for n, (array, row, swap, offset, half) in enumerate(places):
        side, place = spot(swap, offset)
        for b in range(SUB):
            column = pl.multiple_of(place * CHUNK + side * SHARE + half * COLS + b * BLOCK, BLOCK)
            copies.append(
                pltpu.make_async_copy(
                    arrays[array].at[pl.ds(row + b * TOKENS, TOKENS), :],
                    out_ref.at[:, pl.ds(column, BLOCK)],
                    sems.at[n * SUB + b],
                )
            )
            copies[-1].start()
    for n, (array, row, swap, offset, half) in enumerate(places):
        tail_copies[n].wait()
        side, place = spot(swap, offset)
        tail = tails[n].astype(jnp.float32)
        tail = tail[: 2 * SUB] + tail[2 * SUB : 4 * SUB]
        for t in range(2):
            table[place, side, half * SUB : (half + 1) * SUB, t * BLOCK : (t + 1) * BLOCK] = tail[
                t * SUB : (t + 1) * SUB
            ]
    if last:
        for place in range(CHIPS):
            for side in range(2):
                row = (2 * place + side) * 2 * SUB
                scale_ref[row : row + 2 * SUB, :] = table[place, side][:, :TOKENS]
    for copy in copies:
        copy.wait()


def assemble(index, arrays, places, before, last):
    table_shape = (CHIPS, 2, 2 * SUB, 2 * BLOCK)
    out_shape = [jax.ShapeDtypeStruct((TOKENS, D), jnp.bfloat16)]
    out_shape.append(
        jax.ShapeDtypeStruct((D // BLOCK, TOKENS) if last else table_shape, jnp.float32)
    )
    scratch = [pltpu.VMEM(table_shape, jnp.float32)] if last else []
    fresh = before is None
    return pl.pallas_call(
        functools.partial(assemble_kernel, places, fresh, last),
        out_shape=tuple(out_shape),
        in_specs=[SMEM] + [ANY] * len(arrays) + ([] if fresh else [ANY, VMEM]),
        out_specs=(ANY, VMEM),
        scratch_shapes=scratch
        + [
            pltpu.VMEM((len(places), 16, BLOCK), jnp.bfloat16),
            pltpu.SemaphoreType.DMA((len(places) * SUB,)),
            pltpu.SemaphoreType.DMA((len(places),)),
        ],
        input_output_aliases={} if fresh else {len(arrays) + 1: 0},
        compiler_params=pltpu.CompilerParams(vmem_limit_bytes=4 << 20),
        cost_estimate=pl.CostEstimate(flops=1 << 20, bytes_accessed=4 << 20, transcendentals=0),
        name="assemble",
    )(index, *arrays, *([] if fresh else before))


def add(arrived, own):
    return (arrived.astype(jnp.float32) + own.astype(jnp.float32)).astype(jnp.bfloat16)


def send(x, pairs):
    return lax.ppermute(x, "tp", pairs)


def layer(queries, keys, values, out_weight, signs):
    ctx, tp = lax.axis_index("ctx"), lax.axis_index("tp")
    core, chip = tp & 1, tp >> 1

    place = jnp.stack(
        [ctx * TOKENS, core, chip, ctx >> 2, ctx & 3, 1 - 2 * (chip & 1)]
    ).astype(jnp.int32)

    other_weight = send(out_weight, PAIR)

    def spread_out(x, pairs):
        came = [lax.ppermute(x, ("ctx", "tp"), way) for way in pairs]
        return jnp.concatenate([x, *came], 0)

    key_part = lax.dynamic_slice_in_dim(keys, chip * HEAD, HEAD, 1)
    value_part = lax.dynamic_slice_in_dim(values, chip * HEAD, HEAD, 1)
    held = spread_out(jnp.where(core == 0, key_part, value_part), FIRST)
    held = spread_out(held, SECOND)
    swapped = send(held, PAIR)

    turn = jnp.asarray(turn_matrix(), jnp.bfloat16)
    gatherer = jnp.asarray(gather_matrix(), jnp.bfloat16)
    attended = attention(place, queries, held, swapped)
    parts = project(
        place,
        attended,
        send(attended, PAIR),
        out_weight,
        other_weight,
        signs[None, :],
        turn,
        gatherer,
    )

    def exchange(for_a, for_b):
        came_b = send(for_a, WAY_A)
        came_a = send(for_b, WAY_B)
        return came_a, came_b

    def part(distance, way, half):
        return parts[half if distance == 4 else 2 + 4 * (3 - distance) + 2 * way + half]

    came = {}
    for step, (distance, half) in enumerate(((4, 0), (3, 0), (3, 1), (2, 1), (2, 0), (1, 0), (1, 1))):
        for_a, for_b = part(distance, 0, half), part(distance, 1, 1 - half)
        if step >= 2:
            came_a, came_b = lax.optimization_barrier(came[step - 2])
            for_a, for_b = add(came_a, for_a), add(came_b, for_b)
        came[step] = exchange(for_a, for_b)
    packed = pack(parts[14], (came[6][0], came[5][1]), (came[5][0], came[6][1]))

    steps, place_of = [], []
    sends = [((packed[0], 0), (packed[1], 1)), ((packed[1], 1), (packed[0], 0))]
    for step in range(7):
        (for_a, half_a), (for_b, half_b) = sends[step]
        for_a, for_b = lax.optimization_barrier((for_a, for_b))
        came_a, came_b = exchange(for_a, for_b)
        sends.append(((came_a, half_b), (came_b, half_a)))
        hop = step // 2 + 1
        steps.append((came_a, came_b))
        place_of.append(((-hop, half_b), (hop, half_a)))
    steps.insert(0, tuple(packed))
    place_of.insert(0, ((0, 0), (0, 1)))
    swapped = []
    for pieces in steps:
        joined = jnp.concatenate(pieces, 0)
        swapped.append(send(joined, PAIR))

    def gather(mine, theirs, before, last=False):
        arrays, places = [], []
        for step in mine:
            for piece, spot in zip(steps[step], place_of[step]):
                places.append((len(arrays), 0, False, *spot))
                arrays.append(piece)
        for step in theirs:
            for row, spot in zip((0, MSG), place_of[step]):
                places.append((len(arrays), row, True, *spot))
            arrays.append(swapped[step])
        return assemble(place, arrays, tuple(places), before, last)

    result = gather((0, 1, 2), (0, 1, 2), None)
    result = gather((3, 4), (3, 4), result)
    result = gather((5, 6, 7), (5, 6), result)
    payload, scales = gather((), (7,), result, True)
    return payload, scales.T


def solution(mesh):
    return jax.shard_map(
        layer,
        mesh=mesh,
        in_specs=(P("ctx", "tp"), P("ctx", None), P("ctx", None), P("tp", None), P()),
        out_specs=(P("ctx", None), P("ctx", None)),
        check_vma=False,
    )
```
